32 devices in a mesh: seq: 32 (over z, y, x, core), head: 1.
Axes of the slice: x: 2, y: 2, z: 4, core: 2. Of those that a mesh axis runs over, the one named last changes fastest.
Arguments:
- queries: bfloat16 [8192, 2048], P('seq', 'head'), may hold values from -6 to 6
- key_vectors: bfloat16 [8192, 2048], P('seq', 'head'), may hold values from -6 to 6
- value_vectors: bfloat16 [8192, 2048], P('seq', 'head'), may hold values from -6 to 6
- forget_gates: float32 [8192, 16], P('seq', 'head'), may hold values from 0.4 to 1, as said below
- shard_counts: int32 [32], P('seq'), may hold values from 1 to 256, 6144 in all
- gram_start: float32 [16, 128, 128], P('head'), may hold values from -4 to 12, as said below
- memory_start: float32 [16, 128, 128], P('head'), may hold values from -6 to 6
- ridge_terms: float32 [16, 128], P('head'), may hold values from 0.05 to 1
- norm_gain: float32 [2048], P('head'), may hold values from 0.1 to 1.9
- out_weight: bfloat16 [2048, 2048], P('head'), may hold values from -0.125 to 0.125
Outputs:
- mixed_out: bfloat16 [8192, 2048], P('seq', 'head')
The draws below stay inside these ranges and needn't reach their ends.
Inputs may be any that keep to these rules, and one draw needn't show every extreme that they name: `shard_counts`: slots of a shard at local positions from its count on are padding; at least one shard is full. `forget_gates`: each gate lies in (0, 1]. `gram_start`: each head's matrix is symmetric positive semidefinite.
All inputs are finite; a program needn't handle non-finite values.
Results may differ from the reference program's by a relative error of at most 0.02.
Values may be sent and summed in bfloat16 or wider, within the bound.
No kernel may reach another device: no remote copies, remote signals or barrier semaphores. Data moves between devices by JAX's collectives and lax.ppermute only.
A program may use at most 128 MiB of HBM per device.

```python
import math
import jax
import jax.numpy as jnp
import numpy as np
from jax import lax

D = 2048
HEAD_COUNT = 16
HEAD_DIMENSION = 128
TOK_DEV = 256
ITERS = 16
TOKEN_SLOTS = 8192
N_SEQ = 32
N_HEAD = 1


def draw_gram_start(key, part):
    spanning_rows = jax.random.normal(key, (HEAD_COUNT, 4 * HEAD_DIMENSION, HEAD_DIMENSION), jnp.float32)
    return jnp.einsum('cgy,cgl->cyl', spanning_rows, spanning_rows, precision=lax.Precision.HIGHEST) / HEAD_DIMENSION


def head_order(head_key):
    return jax.random.permutation(head_key, HEAD_DIMENSION)


def draw_key_vectors(key, part):
    key_sequence = jax.random.split(key, 3)
    group_width = max(HEAD_DIMENSION // 8, 1)
    group_total = HEAD_DIMENSION // group_width
    orderings = jax.vmap(head_order)(jax.random.split(key_sequence[0], HEAD_COUNT))
    positions = jnp.argsort(orderings, axis=-1).astype(jnp.int32)
    group_index = positions // group_width
    head_offset = jax.random.randint(key_sequence[1], (HEAD_COUNT,), 0, group_total)
    shard_index = jnp.arange(TOKEN_SLOTS, dtype=jnp.int32) // TOK_DEV
    chosen_group = (shard_index[:, None] + head_offset[None, :]) % group_total
    favoured = group_index[None, :, :] == chosen_group[:, :, None]
    spread_scale = jnp.where(favoured, 1.5, 0.2)
    base_values = jax.random.normal(key_sequence[2], (TOKEN_SLOTS, HEAD_COUNT, HEAD_DIMENSION), jnp.float32)
    shaped = jnp.clip(base_values * spread_scale, -6.0, 6.0)
    return shaped.reshape(TOKEN_SLOTS, HEAD_COUNT * HEAD_DIMENSION).astype(jnp.bfloat16)


def draw_forget_gates(key, part):
    key_sequence = jax.random.split(key, 8)
    order_rank = jnp.argsort(jax.random.permutation(key_sequence[0], HEAD_COUNT)).astype(jnp.int32)
    slow_count = HEAD_COUNT // 2
    medium_count = 5 * HEAD_COUNT // 16
    slow_heads = order_rank < slow_count
    medium_heads = jnp.logical_and(order_rank >= slow_count, order_rank < slow_count + medium_count)
    fast_rate = jnp.exp(jax.random.uniform(key_sequence[1], (HEAD_COUNT,), jnp.float32, math.log(1.0 / 50.0), math.log(1.0 / 30.0)))
    slow_rate = jnp.exp(jax.random.uniform(key_sequence[2], (HEAD_COUNT,), jnp.float32, math.log(0.1), math.log(0.4))) / TOKEN_SLOTS
    medium_rate = jnp.exp(jax.random.uniform(key_sequence[7], (HEAD_COUNT,), jnp.float32, math.log(math.log(4.0)), math.log(math.log(10.0)))) / TOK_DEV
    per_head_rate = jnp.where(slow_heads, slow_rate, jnp.where(medium_heads, medium_rate, fast_rate))
    block_factor = jnp.exp(jax.random.uniform(key_sequence[3], (TOKEN_SLOTS // TOK_DEV, HEAD_COUNT), jnp.float32, math.log(0.5), math.log(2.0)))
    block_factor = jnp.repeat(block_factor, TOK_DEV, axis=0)
    small_perturbation = jax.random.uniform(key_sequence[4], (TOKEN_SLOTS, HEAD_COUNT), jnp.float32, 0.5, 1.5)
    marked_locations = jax.random.randint(key_sequence[5], (2, HEAD_COUNT), 0, TOKEN_SLOTS)
    token_place = jnp.arange(TOKEN_SLOTS, dtype=jnp.int32)
    spike_selected = jnp.any(token_place[:, None, None] == marked_locations[None, :, :], axis=1)
    spike_retain = jax.random.uniform(key_sequence[6], (TOKEN_SLOTS, HEAD_COUNT), jnp.float32, 0.5, 0.8)
    return jnp.exp(-per_head_rate[None, :] * block_factor * small_perturbation) * jnp.where(spike_selected, spike_retain, 1.0)


def level_of(key, dims, cuts, smallest, high):
    level = 1.0
    for dim, blocks in cuts:
        draws = jax.random.uniform(jax.random.fold_in(jax.random.fold_in(key, 6), dim), (blocks,), jnp.float32, smallest / len(cuts), high / len(cuts))
        level = level * jnp.repeat(jnp.exp(draws), dims[dim] // blocks).reshape((-1,) + (1,) * (len(dims) - 1 - dim))
    return level


def length_profile(count, total, bound, skew):
    loads = [(1 << 20) // math.isqrt(rank ** skew) + 1 for rank in range(2, count + 1)]
    spare, given = total - bound - (count - 1), [1] * (count - 1)
    while spare > 0:
        free = [i for i in range(count - 1) if given[i] < bound]
        whole, remaining = sum([loads[i] for i in free]), spare
        for i in free:
            addition = min(bound - given[i], max(1, remaining * loads[i] // whole), spare)
            given[i] = given[i] + addition
            spare = spare - addition
    return np.array([bound] + given)


def ragged(rng, number_of, total, limit, lean):
    if number_of == 2:
        one = jax.random.randint(rng, (), max(1, total - limit), min(limit, total - 1) + 1)
        return jnp.stack([one, total - one])
    sizes = jnp.asarray(length_profile(number_of, total, limit, lean), jnp.int32)
    couples = (number_of - 1) // 2
    donor, taker = sizes[1:1 + 2 * couples:2], sizes[2:2 + 2 * couples:2]
    slack = jnp.minimum(donor - 1, limit - taker)
    moved = jax.random.randint(jax.random.fold_in(rng, 1), (couples,), 0, 1 << 20) % (slack + 1)
    sizes = sizes.at[1:1 + 2 * couples:2].set(donor - moved).at[2:2 + 2 * couples:2].set(taker + moved)
    return sizes[jax.random.permutation(jax.random.fold_in(rng, 2), number_of)]


def gaussian(stream_key, extent, spread, most, cuts=(), kind=jnp.bfloat16):
    level = level_of(stream_key, extent, cuts, -0.22, 0.18) if cuts else 1.0
    values = jax.random.normal(stream_key, extent, jnp.float32) * spread * level
    return jnp.minimum(jnp.maximum(values, -most), most).astype(kind)


def setup_inputs(seed: int = 0) -> dict:
    seeds = jax.random.split(jax.random.key(seed), 11)
    return {
        "queries": gaussian(seeds[0], (TOKEN_SLOTS, HEAD_COUNT * HEAD_DIMENSION), 1.0, 6.0, ((0, 32),)),
        "key_vectors": draw_key_vectors(jax.random.fold_in(seeds[10], 71), 0),
        "value_vectors": gaussian(seeds[2], (TOKEN_SLOTS, HEAD_COUNT * HEAD_DIMENSION), 1.0, 6.0, ((0, 32),)),
        "forget_gates": draw_forget_gates(jax.random.fold_in(seeds[10], 71), 0),
        "shard_counts": ragged(seeds[4], N_SEQ, N_SEQ * TOK_DEV * 3 // 4, TOK_DEV, 0).astype(jnp.int32),
        "gram_start": draw_gram_start(jax.random.fold_in(seeds[10], 71), 0),
        "memory_start": gaussian(seeds[6], (HEAD_COUNT, HEAD_DIMENSION, HEAD_DIMENSION), 1.0, 6.0, (), jnp.float32),
        "ridge_terms": jnp.clip(jnp.exp(jax.random.uniform(seeds[7], (HEAD_COUNT, HEAD_DIMENSION), jnp.float32, math.log(0.05), math.log(1.0))), 0.05, 1.0),
        "norm_gain": jnp.clip(1.0 + 0.18 * jax.random.normal(seeds[8], (HEAD_COUNT * HEAD_DIMENSION,), jnp.float32), 0.1, 1.9),
        "out_weight": gaussian(seeds[9], (HEAD_COUNT * HEAD_DIMENSION, D), (HEAD_COUNT * HEAD_DIMENSION) ** -0.5, 0.125),
    }


precise = lax.Precision.HIGHEST

def unit_rows(matrix):
    return matrix * lax.rsqrt(lax.optimization_barrier(jnp.sum(matrix * matrix, axis=-1, keepdims=True)) + 1e-06)

def summarize(key_rows, value_rows, running):
    tail_decay = jnp.exp(running[:, -1:] - running)[..., None]
    weighted = key_rows * tail_decay
    gram_local = jnp.einsum('hcd,hce->hde', weighted, key_rows, precision=precise)
    memory_local = jnp.einsum('hce,hcd->hed', value_rows, weighted, precision=precise)
    return (jnp.exp(running[:, -1]), gram_local, memory_local)

def solve_block(query_rows, key_rows, value_rows, running, gram_prev, memory_prev, ridge_terms):
    span_rows = running.shape[1]
    log_gaps = running[:, :, None] - running[:, None, :]
    lower_mask = lax.iota(jnp.int32, span_rows)[:, None] >= lax.iota(jnp.int32, span_rows)[None, :]
    within_block = jnp.where(lower_mask[None], jnp.exp(jnp.minimum(log_gaps, 0.0)), 0.0)
    lead_decay = jnp.exp(running)[..., None]
    ridge_diag = ridge_terms[:, None, :]

    def apply_op(vector_in, state_mat, rows_in):
        near_terms = jnp.einsum('hcd,hsd->hcs', vector_in, key_rows, precision=precise) * within_block
        return lead_decay * jnp.einsum('hcd,hed->hce', vector_in, state_mat, precision=precise) + jnp.einsum('hcs,hse->hce', near_terms, rows_in, precision=precise)

    def cg_step(loop_index, state_tuple):
        answer, residual, direction, norm_now = state_tuple
        image_vec = apply_op(direction, gram_prev, key_rows) + ridge_diag * direction
        step_size = norm_now / lax.optimization_barrier(jnp.sum(direction * image_vec, axis=-1, keepdims=True))
        answer = answer + step_size * direction
        residual = residual - step_size * image_vec
        norm_next = lax.optimization_barrier(jnp.sum(residual * residual, axis=-1, keepdims=True))
        direction = residual + norm_next / norm_now * direction
        return (answer, residual, direction, norm_next)
    initial = (jnp.zeros_like(query_rows), query_rows, query_rows, lax.optimization_barrier(jnp.sum(query_rows * query_rows, axis=-1, keepdims=True)))
    answer = lax.fori_loop(0, ITERS, cg_step, initial)[0]
    return apply_op(answer, memory_prev, value_rows)

def reference(queries, key_vectors, value_vectors, forget_gates, shard_counts, gram_start, memory_start, ridge_terms, norm_gain, out_weight):
    token_place = jnp.arange(TOKEN_SLOTS, dtype=jnp.int32)
    shard_of = (token_place // TOK_DEV).astype(jnp.int32)
    live_rows = (token_place % TOK_DEV < shard_counts[shard_of]).astype(jnp.float32)[:, None]

    def split_heads(matrix):
        return jnp.transpose(matrix.astype(jnp.float32).reshape(N_SEQ, TOK_DEV, HEAD_COUNT, HEAD_DIMENSION), (0, 2, 1, 3))
    live_blocks = live_rows.reshape(N_SEQ, 1, TOK_DEV, 1)
    query_rows = unit_rows(split_heads(queries))
    key_rows = unit_rows(split_heads(key_vectors)) * live_blocks
    value_rows = split_heads(value_vectors) * live_blocks
    log_decay = jnp.where(live_rows > 0, jnp.log(forget_gates), 0.0)
    log_decay = jnp.transpose(log_decay.reshape(N_SEQ, TOK_DEV, HEAD_COUNT), (0, 2, 1))
    running = jnp.cumsum(log_decay, axis=2)

    def shard_step(carried, inputs_now):
        gram_prev, memory_prev = carried
        query_block, key_block, value_block, running_block = inputs_now
        output = solve_block(query_block, key_block, value_block, running_block, gram_prev, memory_prev, ridge_terms)
        decay_total, gram_local, memory_local = summarize(key_block, value_block, running_block)
        gram_next = decay_total[:, None, None] * gram_prev + gram_local
        memory_next = decay_total[:, None, None] * memory_prev + memory_local
        return ((gram_next, memory_next), output)
    result = lax.scan(shard_step, (gram_start, memory_start), (query_rows, key_rows, value_rows, running))[1]
    scaled = result * lax.rsqrt(lax.optimization_barrier(jnp.mean(result * result, axis=-1, keepdims=True)) + 1e-05)
    flat_rows = jnp.transpose(scaled, (0, 2, 1, 3)).reshape(TOKEN_SLOTS, HEAD_COUNT * HEAD_DIMENSION) * norm_gain[None, :] * live_rows
    normalized = flat_rows.astype(jnp.bfloat16)
    group_width = HEAD_COUNT * HEAD_DIMENSION // N_HEAD
    mixed_sum = jnp.zeros((TOKEN_SLOTS, D), jnp.float32)
    for group_index in range(N_HEAD):
        lo_col = group_index * group_width
        partial_value = jnp.dot(normalized[:, lo_col:lo_col + group_width], out_weight[lo_col:lo_col + group_width], preferred_element_type=jnp.float32)
        rounded = lax.optimization_barrier(partial_value.astype(jnp.bfloat16))
        mixed_sum = mixed_sum + rounded.astype(jnp.float32)
    return mixed_sum.astype(jnp.bfloat16)
```

```python
import functools

import jax
import jax.numpy as jnp
from jax import lax
from jax.experimental import pallas as pl
from jax.experimental.pallas import tpu as pltpu
from jax.sharding import PartitionSpec as P

ITERS = 16
FINE = 9
F = jnp.float32
B = jnp.bfloat16
DEAD = 1e30
VMEM_BYTES = 56 << 20


def split(a):
    hi = a.astype(B)
    return hi, (a - hi.astype(F)).astype(B)


def dot(a, b):
    return jnp.dot(a, b, preferred_element_type=F)


def spec(block, index):
    return pl.BlockSpec(block, index)


def whole(shape):
    zeros = (0,) * len(shape)
    return pl.BlockSpec(shape, lambda *_: zeros)


SMEM = pl.BlockSpec(memory_space=pltpu.SMEM)


def params():
    return pltpu.CompilerParams(vmem_limit_bytes=VMEM_BYTES)


def gates_kernel(count, gates, run_out, wide):
    tokens, heads = gates.shape
    at = lax.broadcasted_iota(jnp.int32, (tokens, heads), 0)
    logs = jnp.where(at < count[0], jnp.log(gates[...]), 0.0)
    wide[...] = jnp.zeros_like(wide)
    wide[:, :heads] = logs
    row = lax.broadcasted_iota(jnp.int32, (tokens, tokens), 0)
    col = lax.broadcasted_iota(jnp.int32, (tokens, tokens), 1)
    upper = (row <= col).astype(F)
    run_out[...] = jnp.dot(
        wide[...].T[:heads], upper, preferred_element_type=F, precision=lax.Precision.HIGHEST
    )


def gates_call(count, gates):
    tokens, heads = gates.shape
    return pl.pallas_call(
        gates_kernel,
        in_specs=[SMEM, whole(gates.shape)],
        out_specs=whole((heads, tokens)),
        out_shape=jax.ShapeDtypeStruct((heads, tokens), F),
        scratch_shapes=[pltpu.VMEM((tokens, 128), F)],
        name="gates",
    )(count, gates)


def sums_kernel(chunk, width, gram, count, keys, others, run, sums_out, pay_out, keyt_out, norm_out):
    tokens = keys.shape[0]
    at = lax.broadcasted_iota(jnp.int32, (1, tokens), 1)
    live = (at < count[0]).astype(F)
    for j in range(chunk):
        cols = slice(j * width, (j + 1) * width)
        key = keys[:, cols]
        keyt = key.astype(F).T
        square = jnp.sum(keyt * keyt, axis=0, keepdims=True) + 1e-06
        now = run[j : j + 1, :]
        last = now[:, tokens - 1 :]
        tail = jnp.exp(last - now) * live
        if gram:
            left = keyt * (tail / square)
            keyt_out[j] = keyt.astype(B)
            norm_out[j : j + 1, :] = square
        else:
            left = others[:, cols].astype(F).T * (tail * lax.rsqrt(square))
        hi, lo = split(left)
        both = dot(jnp.concatenate([hi, lo], 1), jnp.concatenate([key, key], 0))
        sums_out[j, :width] = both
        pay_out[j, :width] = both.astype(B)
        decay = jnp.broadcast_to(jnp.exp(last), (1, width))
        first = decay.astype(B)
        second, third = split(decay - first.astype(F))
        sums_out[j, width:] = jnp.broadcast_to(decay, (8, width))
        row = lax.broadcasted_iota(jnp.int32, (16, width), 0)
        pay_out[j, width:] = jnp.where(
            row == 0,
            first.astype(F),
            jnp.where(row == 1, second.astype(F), jnp.where(row == 2, third.astype(F), 0.0)),
        ).astype(B)


def sums_call(count, keys, others, run, chunk, place, gram):
    tokens = keys.shape[0]
    heads = run.shape[0]
    width = keys.shape[1] // heads
    block = spec((tokens, chunk * width), lambda i: (0, place))
    shapes = [
        jax.ShapeDtypeStruct((chunk, width + 8, width), F),
        jax.ShapeDtypeStruct((chunk, width + 16, width), B),
    ]
    if gram:
        shapes += [
            jax.ShapeDtypeStruct((chunk, width, tokens), B),
            jax.ShapeDtypeStruct((chunk, tokens), F),
        ]

    def body(count_ref, keys_ref, *rest):
        if gram:
            run_ref, *outs = rest
            sums_kernel(chunk, width, True, count_ref, keys_ref, None, run_ref, *outs)
        else:
            others_ref, run_ref, *outs = rest
            sums_kernel(chunk, width, False, count_ref, keys_ref, others_ref, run_ref, *outs, None, None)

    mine = run.reshape(heads // chunk, chunk, tokens)[place]
    ins = [count, keys] + ([] if gram else [others]) + [mine]
    return pl.pallas_call(
        body,
        grid=(1,),
        in_specs=[SMEM, block] + ([] if gram else [block]) + [whole(mine.shape)],
        out_specs=[whole(s.shape) for s in shapes],
        out_shape=shapes,
        compiler_params=params(),
        name="gram_sums" if gram else "memory_sums",
    )(*ins)


def decay_of(pay, j, width):
    rows = pay[j, width:].astype(F)
    return rows[0:1] + rows[1:2] + rows[2:3]


def put(pay_out, j, width, total, decay):
    pay_out[j, :width] = total.astype(B)
    first = decay.astype(B)
    second, third = split(decay - first.astype(F))
    row = lax.broadcasted_iota(jnp.int32, (16, width), 0)
    pay_out[j, width:] = jnp.where(
        row == 0,
        first.astype(F),
        jnp.where(row == 1, second.astype(F), jnp.where(row == 2, third.astype(F), 0.0)),
    ).astype(B)


def pair_kernel(half, width, side, own, got, total_out, pay_out):
    c = side[0]
    for j in range(half):
        at = c * half + j
        mine, decay = own[at, :width], own[at, width : width + 1]
        other, other_decay = got[at, :width].astype(F), decay_of(got, at, width)
        total = jnp.where(c == 0, other_decay, 1.0) * mine + jnp.where(c == 0, 1.0, decay) * other
        both = decay * other_decay
        total_out[j, :width] = total
        total_out[j, width:] = jnp.broadcast_to(both, (8, width))
        put(pay_out, j, width, total, both)


def pair_call(side, own, got, half):
    width = own.shape[2]
    shapes = [
        jax.ShapeDtypeStruct((half, width + 8, width), F),
        jax.ShapeDtypeStruct((half, width + 16, width), B),
    ]
    return pl.pallas_call(
        functools.partial(pair_kernel, half, width),
        in_specs=[SMEM, whole(own.shape), whole(got.shape)],
        out_specs=[whole(s.shape) for s in shapes],
        out_shape=shapes,
        compiler_params=params(),
        name="pair",
    )(side, own, got)


def group_kernel(radix, half, width, first, side, own, *rest):
    gots = rest[: radix - 1]
    rest = rest[radix - 1 :]
    if first:
        before = None
        total_out, pay_out, before_out = rest
    else:
        before, total_out, pay_out, before_out = rest
    p = side[0]
    for j in range(half):
        terms = [own[j, :width]] + [g[j, :width].astype(F) for g in gots]
        decays = [own[j, width : width + 1]] + [decay_of(g, j, width) for g in gots]
        total = jnp.zeros_like(terms[0])
        prefix = jnp.zeros_like(terms[0])
        prefix_decay = jnp.ones_like(decays[0])
        for m in range(radix):
            k = p ^ m
            coef = jnp.ones_like(decays[0])
            lead = jnp.ones_like(decays[0])
            for n in range(radix):
                if n != m:
                    o = p ^ n
                    coef = coef * jnp.where(o > k, decays[n], 1.0)
                    if n != 0:
                        lead = lead * jnp.where((o > k) & (o < p), decays[n], 1.0)
            total = total + coef * terms[m]
            if m != 0:
                prefix = prefix + jnp.where(k < p, lead, 0.0) * terms[m]
                prefix_decay = prefix_decay * jnp.where(k < p, decays[m], 1.0)
        every = decays[0]
        for n in range(1, radix):
            every = every * decays[n]
        if not first:
            inner = before[j, width : width + 1]
            prefix = inner * prefix + before[j, :width]
            prefix_decay = inner * prefix_decay
        total_out[j, :width] = total
        total_out[j, width:] = jnp.broadcast_to(every, (8, width))
        put(pay_out, j, width, total, every)
        before_out[j, :width] = prefix
        before_out[j, width:] = jnp.broadcast_to(prefix_decay, (8, width))


def group_call(side, own, gots, before):
    half, _, width = own.shape
    shapes = [
        jax.ShapeDtypeStruct((half, width + 8, width), F),
        jax.ShapeDtypeStruct((half, width + 16, width), B),
        jax.ShapeDtypeStruct((half, width + 8, width), F),
    ]
    ins = [side, own, *gots] + ([] if before is None else [before])
    return pl.pallas_call(
        functools.partial(group_kernel, len(gots) + 1, half, width, before is None),
        in_specs=[SMEM] + [whole(a.shape) for a in ins[1:]],
        out_specs=[whole(s.shape) for s in shapes],
        out_shape=shapes,
        compiler_params=params(),
        name="group",
    )(*ins)


def last_kernel(radix, half, width, first, side, start, *rest):
    gots = rest[: radix - 1]
    before = None if first else rest[radix - 1]
    out = rest[-1]
    p = side[1]
    base = side[0] * half
    for j in range(half):
        prefix = jnp.zeros((width, width), F)
        gone = jnp.ones((1, width), F)
        for m, g in enumerate(gots, 1):
            prefix = prefix + gone * g[j, :width].astype(F)
            gone = gone * jnp.where(p >= m, decay_of(g, j, width), 1.0)
        total = gone * start[base + j] + prefix
        if not first:
            total = before[j, width : width + 1] * total + before[j, :width]
        out[j] = total


def last_call(side, start, gots, before, chunk, place):
    half, _, width = gots[0].shape
    ins = [side, start, *gots] + ([] if before is None else [before])
    block = spec((chunk, width, width), lambda i: (place, 0, 0))
    return pl.pallas_call(
        functools.partial(last_kernel, len(gots) + 1, half, width, before is None),
        grid=(1,),
        in_specs=[SMEM, block] + [whole(a.shape) for a in ins[2:]],
        out_specs=whole((half, width, width)),
        out_shape=jax.ShapeDtypeStruct((half, width, width), F),
        compiler_params=params(),
        name="last",
    )(*ins)


def radices(count):
    rest = count // 2
    out = []
    while rest > 1:
        step = 4 if rest % 4 == 0 else 2
        out.append(step)
        rest //= step
    return out


def prefix(sums, pay, start, count, chunk, place):
    me = lax.axis_index("seq").astype(jnp.int32)
    half = chunk // 2

    def send(a, moves):
        return lax.ppermute(a, "seq", moves)

    got = send(pay, [(i, i ^ 1) for i in range(count)])
    first = got
    side = jnp.stack([me & 1])
    total, pay = pair_call(side, sums, got, half)
    before = None
    stride = 2
    steps = radices(count)
    for n, radix in enumerate(steps):
        spot = (me // stride) % radix
        if n < len(steps) - 1:
            gots = [
                send(pay, [(i, i ^ (m * stride)) for i in range(count)]) for m in range(1, radix)
            ]
            total, pay, before = group_call(jnp.stack([spot]), total, gots, before)
        else:
            gots = [
                send(pay, [(i, i + m * stride) for i in range(count - m * stride)])
                for m in range(1, radix)
            ]
            mine = last_call(jnp.stack([me & 1, spot]), start, gots, before, chunk, place)
        stride *= radix
    theirs = send(mine, [(i, i ^ 1) for i in range(count)])
    return mine, theirs, first


def state_of(c, j, half, width, mine, theirs, first):
    at = j % half
    same = c == j // half
    before = jnp.where(same, mine[at], theirs[at])
    decay = jnp.where(c == 0, 1.0, decay_of(first, j, width))
    local = jnp.where(c == 0, 0.0, first[j, :width].astype(F))
    return decay * before + local


def weights_kernel(chunk, width, count, queries, run, norm, weight_out, query_out, wide):
    tokens = queries.shape[0]
    at = lax.broadcasted_iota(jnp.int32, (1, tokens), 1)
    now = run[...]
    wide[...] = jnp.zeros_like(wide)
    wide[:chunk] = jnp.where(at < count[0], now + jnp.log(norm[...]), DEAD)
    tall = wide[...].T
    row = lax.broadcasted_iota(jnp.int32, (tokens, tokens), 0)
    col = lax.broadcasted_iota(jnp.int32, (tokens, tokens), 1)
    for j in range(chunk):
        weight_out[j] = jnp.where(row <= col, jnp.exp(now[j : j + 1] - tall[:, j : j + 1]), 0.0)
        q = queries[:, j * width : (j + 1) * width].astype(F).T
        query_out[j] = q * lax.rsqrt(jnp.sum(q * q, axis=0, keepdims=True) + 1e-06)


def weights_call(count, queries, run, norm, chunk, place):
    tokens = queries.shape[0]
    heads = run.shape[0]
    width = queries.shape[1] // heads
    mine = run.reshape(heads // chunk, chunk, tokens)[place]
    shapes = [
        jax.ShapeDtypeStruct((chunk, tokens, tokens), F),
        jax.ShapeDtypeStruct((chunk, width, tokens), F),
    ]
    return pl.pallas_call(
        functools.partial(weights_kernel, chunk, width),
        grid=(1,),
        in_specs=[
            SMEM,
            spec((tokens, chunk * width), lambda i: (0, place)),
            whole(mine.shape),
            whole(norm.shape),
        ],
        out_specs=[whole(s.shape) for s in shapes],
        out_shape=shapes,
        scratch_shapes=[pltpu.VMEM((128, tokens), F)],
        compiler_params=params(),
        name="weights",
    )(count, queries, mine, norm)


def solve_kernel(
    chunk, width, side, keys, keyt, queries, weights, run, ridge, mine, theirs, first,
    answer_out, left, dirs, resid, near_top, near_low, far,
):
    tokens = keys.shape[0]
    half_t = tokens // 2
    c = side[0]
    lead = []
    norms = []
    for j in range(chunk):
        key = keys[:, j * width : (j + 1) * width]
        left[j, :tokens, :width] = key
        left[j, :tokens, width:] = key
        gram = state_of(c, j, chunk // 2, width, mine, theirs, first).astype(B)
        left[j, tokens:, :width] = gram
        left[j, tokens:, width:] = gram
        q = queries[j]
        dirs[j] = q
        resid[j] = q
        answer_out[j] = jnp.zeros_like(q)
        norms.append(jnp.sum(q * q, axis=0, keepdims=True))
        lead.append(jnp.exp(run[j : j + 1, :]))

    def spread(j, fine):
        p = dirs[j]
        if fine:
            hi, lo = split(p)
            image = dot(left[j], jnp.concatenate([hi, lo], 0))
        else:
            image = dot(left[j, :, :width], p.astype(B))
        far[j] = image[tokens:]
        top = image[:half_t] * weights[j, :half_t]
        low = image[half_t:tokens, half_t:] * weights[j, half_t:, half_t:]
        if fine:
            near_top[j, 0], near_top[j, 1] = split(top)
            near_low[j, 0], near_low[j, 1] = split(low)
        else:
            near_top[j, 0] = top.astype(B)
            near_low[j, 0] = low.astype(B)

    def gather(j, fine, norm):
        kt = keyt[j]
        p = dirs[j]
        if fine:
            early = kt[:, :half_t]
            one = dot(
                jnp.concatenate([early, early], 1),
                jnp.concatenate([near_top[j, 0, :, :half_t], near_top[j, 1, :, :half_t]], 0),
            )
            two = dot(
                kt,
                jnp.concatenate(
                    [
                        jnp.concatenate([near_top[j, 0, :, half_t:], near_top[j, 1, :, half_t:]], 1),
                        jnp.concatenate([near_low[j, 0], near_low[j, 1]], 1),
                    ],
                    0,
                ),
            )
            near = jnp.concatenate([one, two[:, :half_t] + two[:, half_t:]], 1)
        else:
            low = near_low[j, 0]
            near = dot(
                kt,
                jnp.concatenate(
                    [near_top[j, 0], jnp.concatenate([jnp.zeros_like(low), low], 1)], 0
                ),
            )
        image = lead[j] * far[j] + near + ridge[j] * p
        step = norm / jnp.sum(p * image, axis=0, keepdims=True)
        answer_out[j] = answer_out[j] + step * p
        r = resid[j] - step * image
        resid[j] = r
        after = jnp.sum(r * r, axis=0, keepdims=True)
        dirs[j] = r + (after / norm) * p
        return after

    cut = max(chunk // 2, 1)
    pairs = list(zip(range(cut), range(cut, chunk)))

    def turn(fine, fine_next):
        def body(_, norms):
            norms = list(norms)
            for a, b in pairs:
                spread(b, fine)
                norms[a] = gather(a, fine, norms[a])
            for a, b in pairs:
                spread(a, fine_next)
                norms[b] = gather(b, fine, norms[b])
            return tuple(norms)

        return body

    for a, _ in pairs:
        spread(a, True)
    norms = lax.fori_loop(0, FINE - 1, turn(True, True), tuple(norms))
    norms = turn(True, False)(0, norms)
    lax.fori_loop(FINE, ITERS, turn(False, False), norms)


def solve_call(side, keys, keyt, queries, weights, run, ridge, state, chunk, place):
    tokens = keys.shape[0]
    heads = run.shape[0]
    width = keys.shape[1] // heads
    mine, theirs, first = state
    here = run.reshape(heads // chunk, chunk, tokens)[place]
    block = spec((tokens, chunk * width), lambda i: (0, place))
    ridge_block = spec((chunk, width, 1), lambda i: (place, 0, 0))
    ins = [side, keys, keyt, queries, weights, here, ridge[..., None], mine, theirs, first]
    return pl.pallas_call(
        functools.partial(solve_body, chunk, width),
        grid=(1,),
        in_specs=[SMEM, block]
        + [whole(a.shape) for a in ins[2:6]]
        + [ridge_block]
        + [whole(a.shape) for a in ins[7:]],
        out_specs=whole((chunk, width, tokens)),
        out_shape=jax.ShapeDtypeStruct((chunk, width, tokens), F),
        scratch_shapes=[
            pltpu.VMEM((chunk, tokens + width, 2 * width), B),
            pltpu.VMEM((chunk, width, tokens), F),
            pltpu.VMEM((chunk, width, tokens), F),
            pltpu.VMEM((chunk, 2, tokens // 2, tokens), B),
            pltpu.VMEM((chunk, 2, tokens // 2, tokens // 2), B),
            pltpu.VMEM((chunk, width, tokens), F),
        ],
        compiler_params=params(),
        name="solve",
    )(*ins)


def solve_body(chunk, width, side, keys, keyt, queries, weights, run, ridge, *rest):
    tokens = keys.shape[0]
    wide = [jnp.broadcast_to(ridge[j], (width, tokens)) for j in range(chunk)]
    solve_kernel(chunk, width, side, keys, keyt, queries, weights, run, wide, *rest)


def readout_kernel(
    chunk, width, pair, side, keys, values, answers, weights, run, norm, gain,
    mine, theirs, first, out_weight, count, into, out, total, state,
):
    tokens = keys.shape[0]
    i = pl.program_id(0)
    c = side[0]

    @pl.when(i == 0)
    def _():
        for j in range(chunk):
            state[j] = state_of(c, j, chunk // 2, width, mine, theirs, first).astype(B)
        total[...] = jnp.zeros_like(total) if into is None else into[...]

    at = lax.broadcasted_iota(jnp.int32, (1, tokens), 1)
    live = (at < count[0]).astype(F)
    rows = []
    for j in range(pair):
        cols = slice(j * width, (j + 1) * width)
        hi, lo = split(answers[j])
        both = jnp.concatenate([hi, lo], 0)
        key = keys[:, cols]
        near = (dot(jnp.concatenate([key, key], 1), both) * weights[j]).astype(B)
        value = (values[:, cols].astype(F).T * jnp.sqrt(norm[j])).astype(B)
        memory = state[i * pair + j]
        o = jnp.exp(run[j]) * dot(jnp.concatenate([memory, memory], 1), both) + dot(value, near)
        scale = lax.rsqrt(jnp.mean(o * o, axis=0, keepdims=True) + 1e-05) * live
        rows.append((o * scale).T * gain[:, cols])
    y = jnp.concatenate(rows, 1).astype(B)
    total[...] += dot(y, out_weight[...])

    @pl.when(i == pl.num_programs(0) - 1)
    def _():
        out[...] = total[...].astype(out.dtype)


def readout_call(
    side, keys, values, answers, weights, run, norm, gain, state, out_weight, count, into, chunk, place, last
):
    tokens = keys.shape[0]
    heads = run.shape[0]
    width = keys.shape[1] // heads
    model = out_weight.shape[1]
    pair = 2 if chunk % 2 == 0 else 1
    turns = chunk // pair
    base = place * turns
    here = run.reshape(heads // chunk, chunk, 1, tokens)[place]
    norm = norm.reshape(chunk, 1, tokens)
    mine, theirs, first = state
    tok = spec((tokens, pair * width), lambda i: (0, base + i))
    row = spec((pair, 1, tokens), lambda i: (i, 0, 0))
    ins = [side, keys, values, answers, weights, here, norm, gain.reshape(1, -1),
           mine, theirs, first, out_weight, count]
    in_specs = [
        SMEM,
        tok,
        tok,
        spec((pair, width, tokens), lambda i: (i, 0, 0)),
        spec((pair, tokens, tokens), lambda i: (i, 0, 0)),
        row,
        row,
        spec((1, pair * width), lambda i: (0, base + i)),
        whole(mine.shape),
        whole(theirs.shape),
        whole(first.shape),
        spec((pair * width, model), lambda i: (base + i, 0)),
        SMEM,
    ]
    if into is not None:
        ins.append(into)
        in_specs.append(whole(into.shape))

    def body(*refs):
        refs = list(refs)
        if into is None:
            refs.insert(13, None)
        readout_kernel(chunk, width, pair, *refs)

    return pl.pallas_call(
        body,
        grid=(turns,),
        in_specs=in_specs,
        out_specs=whole((tokens, model)),
        out_shape=jax.ShapeDtypeStruct((tokens, model), B if last else F),
        scratch_shapes=[
            pltpu.VMEM((tokens, model), F),
            pltpu.VMEM((chunk, width, width), B),
        ],
        compiler_params=params(),
        name="readout",
    )(*ins)


def local(
    shards, columns,
    queries, key_vectors, value_vectors, forget_gates, shard_counts, gram_start,
    memory_start, ridge_terms, norm_gain, out_weight,
):
    heads = forget_gates.shape[1]
    chunk = min(heads, 8)
    parts = range(heads // chunk)
    me = lax.axis_index("seq").astype(jnp.int32)
    side = jnp.stack([me & 1])
    run = gates_call(shard_counts, forget_gates)
    grams = [
        sums_call(shard_counts, key_vectors, None, run, chunk, n, True) for n in parts
    ]
    gram_states = [
        prefix(grams[n][0], grams[n][1], gram_start, shards, chunk, n) for n in parts
    ]
    memories = [
        sums_call(shard_counts, key_vectors, value_vectors, run, chunk, n, False) for n in parts
    ]
    memory_states = [
        prefix(memories[n][0], memories[n][1], memory_start, shards, chunk, n) for n in parts
    ]
    weights = [
        weights_call(shard_counts, queries, run, grams[n][3], chunk, n) for n in parts
    ]
    answers = [
        solve_call(
            side, key_vectors, grams[n][2], weights[n][1], weights[n][0], run, ridge_terms,
            gram_states[n], chunk, n,
        )
        for n in parts
    ]
    mixed = None
    for n in parts:
        mixed = readout_call(
            side, key_vectors, value_vectors, answers[n], weights[n][0], run, grams[n][3],
            norm_gain, memory_states[n], out_weight, shard_counts, mixed, chunk, n,
            n == len(parts) - 1,
        )
    if columns > 1:
        mixed = lax.psum_scatter(mixed, "head", scatter_dimension=1, tiled=True)
    return mixed


def solution(mesh):
    return jax.shard_map(
        functools.partial(local, mesh.shape["seq"], mesh.shape["head"]),
        mesh=mesh,
        in_specs=(
            P("seq", "head"),
            P("seq", "head"),
            P("seq", "head"),
            P("seq", "head"),
            P("seq"),
            P("head", None, None),
            P("head", None, None),
            P("head", None),
            P("head"),
            P("head", None),
        ),
        out_specs=P("seq", "head"),
        check_vma=False,
    )
```

```python
import functools

import jax
import jax.numpy as jnp
from jax import lax
from jax.experimental import pallas as pl
from jax.experimental.pallas import tpu as pltpu
from jax.sharding import PartitionSpec as P

ITERS = 16
FINE = 9
BATCH = 4
F = jnp.float32
B = jnp.bfloat16
DEAD = 1e30
MIB = 1 << 20


def split(a):
    hi = a.astype(B)
    return hi, (a - hi.astype(F)).astype(B)


def dot(a, b):
    return jnp.dot(a, b, preferred_element_type=F)


def spec(block, index):
    return pl.BlockSpec(block, index)


def whole(shape):
    zeros = (0,) * len(shape)
    return pl.BlockSpec(shape, lambda *_: zeros)


SMEM = pl.BlockSpec(memory_space=pltpu.SMEM)


def params(mib):
    return pltpu.CompilerParams(vmem_limit_bytes=mib * MIB)


def cost(us):
    return pl.CostEstimate(flops=int(us * 1e9), bytes_accessed=int(us * 1e6), transcendentals=0)


def split_rows(tail, decay, lead):
    first = decay.astype(B).astype(F)
    second = (decay - first).astype(B).astype(F)
    third = decay - first - second
    row = lax.broadcasted_iota(jnp.int32, tail, 0)
    n = 0
    out = jnp.zeros(tail, F)
    if lead is not None:
        out = jnp.where(row == 0, lead, out)
        n = 1
    for value in (first, second, third):
        out = jnp.where(row == n, value, out)
        n += 1
    return out.astype(B)


def emit(sums_out, pay_out, j, body, decay, lead):
    height = body.shape[0]
    width = body.shape[1]
    sums_out[j, :height] = body
    pay_out[j, :height] = body.astype(B)
    row = lax.broadcasted_iota(jnp.int32, (16, width), 0)
    wide = jnp.broadcast_to(decay, (16, width))
    sums_out[j, height:] = wide if lead is None else jnp.where(row == 0, lead, wide)
    pay_out[j, height:] = split_rows((16, width), wide, lead)


def pack(gram):
    half = gram.shape[0] // 2
    turned = pltpu.roll(gram[half:], half, 1)
    row = lax.broadcasted_iota(jnp.int32, turned.shape, 0)
    col = lax.broadcasted_iota(jnp.int32, turned.shape, 1)
    body = jnp.where((col < half) & (row < col), turned, gram[:half])
    diagonal = jnp.sum(jnp.where(row == col, turned, 0.0), axis=0, keepdims=True)
    return body, diagonal


def unpack(body, diagonal):
    half, width = body.shape
    flipped = jnp.concatenate([body, jnp.zeros_like(body)], 0).T
    row = lax.broadcasted_iota(jnp.int32, body.shape, 0)
    col = lax.broadcasted_iota(jnp.int32, body.shape, 1)
    top = jnp.where((col < half) & (row < col), flipped[:half], body)
    corner = jnp.where(row < col, body, jnp.where(row == col, diagonal, flipped[:half]))
    low = jnp.where(col < half, flipped[half:], pltpu.roll(corner, half, 1))
    return jnp.concatenate([top, low], 0)


def gram_kernel(chunk, width, count, gates, keys, sums_out, pay_out, keyt_out, run_out, square_out):
    tokens = keys.shape[0]
    at = lax.broadcasted_iota(jnp.int32, (1, tokens), 1)
    live = at < count[0]
    row = lax.broadcasted_iota(jnp.int32, (tokens, tokens), 0)
    col = lax.broadcasted_iota(jnp.int32, (tokens, tokens), 1)
    run = jnp.dot(
        jnp.where(live, jnp.log(gates[...]), 0.0),
        (row <= col).astype(F),
        preferred_element_type=F,
        precision=lax.Precision.HIGHEST,
    )
    run_out[...] = run
    for j in range(chunk):
        key = keys[:, j * width : (j + 1) * width]
        keyt = key.astype(F).T
        square = jnp.sum(keyt * keyt, axis=0, keepdims=True) + 1e-06
        now = run[j : j + 1]
        last = now[:, tokens - 1 :]
        tail = jnp.where(live, jnp.exp(last - now), 0.0)
        keyt_out[j] = keyt.astype(B)
        square_out[j : j + 1, :] = square
        hi, lo = split(keyt * (tail / square))
        gram = dot(jnp.concatenate([hi, lo], 1), jnp.concatenate([key, key], 0))
        body, diagonal = pack(gram)
        emit(sums_out, pay_out, j, body, jnp.broadcast_to(jnp.exp(last), (1, width)), diagonal)


def gram_call(count, gates, keys, chunk, place):
    tokens = keys.shape[0]
    width = keys.shape[1] // gates.shape[0]
    rows = width // 2 + 16
    shapes = [
        jax.ShapeDtypeStruct((chunk, rows, width), F),
        jax.ShapeDtypeStruct((chunk, rows, width), B),
        jax.ShapeDtypeStruct((chunk, width, tokens), B),
        jax.ShapeDtypeStruct((chunk, tokens), F),
        jax.ShapeDtypeStruct((chunk, tokens), F),
    ]
    return pl.pallas_call(
        functools.partial(gram_kernel, chunk, width),
        grid=(1,),
        in_specs=[
            SMEM,
            spec((chunk, tokens), lambda i: (place, 0)),
            spec((tokens, chunk * width), lambda i: (0, place)),
        ],
        out_specs=[whole(s.shape) for s in shapes],
        out_shape=shapes,
        compiler_params=params(16),
        cost_estimate=cost(3),
        name="gram_sums",
    )(count, gates, keys)


def memory_kernel(chunk, width, count, run, square, keys, values, sums_out, pay_out):
    tokens = keys.shape[0]
    at = lax.broadcasted_iota(jnp.int32, (1, tokens), 1)
    live = at < count[0]
    for j in range(chunk):
        cols = slice(j * width, (j + 1) * width)
        key = keys[:, cols]
        now = run[j : j + 1]
        last = now[:, tokens - 1 :]
        tail = jnp.where(live, jnp.exp(last - now), 0.0)
        hi, lo = split(values[:, cols].astype(F).T * (tail * lax.rsqrt(square[j : j + 1])))
        memory = dot(jnp.concatenate([hi, lo], 1), jnp.concatenate([key, key], 0))
        emit(sums_out, pay_out, j, memory, jnp.broadcast_to(jnp.exp(last), (1, width)), None)


def memory_call(count, run, square, keys, values, width, place):
    tokens = keys.shape[0]
    chunk = run.shape[0]
    block = spec((tokens, chunk * width), lambda i: (0, place))
    shapes = [
        jax.ShapeDtypeStruct((chunk, width + 16, width), F),
        jax.ShapeDtypeStruct((chunk, width + 16, width), B),
    ]
    return pl.pallas_call(
        functools.partial(memory_kernel, chunk, width),
        grid=(1,),
        in_specs=[SMEM, whole(run.shape), whole(square.shape), block, block],
        out_specs=[whole(s.shape) for s in shapes],
        out_shape=shapes,
        compiler_params=params(16),
        cost_estimate=cost(3),
        name="memory_sums",
    )(count, run, square, keys, values)


def decay_in(got, data):
    parts = [got[:, data + n : data + n + 1].astype(F) for n in range(3)]
    return parts[0] + parts[1] + parts[2]


def payload(total, data):
    row = lax.broadcasted_iota(jnp.int32, total.shape, 1)
    first = lax.reduce_precision(total, 8, 7)
    second = lax.reduce_precision(total - first, 8, 7)
    third = total - first - second
    return jnp.where(
        row <= data, total, jnp.where(row == data + 1, total - first, jnp.where(row == data + 2, third, 0.0))
    ).astype(B)


def after(a, *others):
    return lax.optimization_barrier((a, *others))[0]


def prefix(sums, pay, data, shards):
    me = lax.axis_index("seq").astype(jnp.int32)
    half = sums.shape[0] // 2
    first = lax.ppermute(pay, "seq", [(i, i ^ 1) for i in range(shards)])
    late = yield pay
    first = after(first, *late)
    low = (me & 1) == 0
    total = jnp.where(low, sums[:half], sums[half:])
    got = jnp.where(low, first[:half], first[half:])
    row = lax.broadcasted_iota(jnp.int32, total.shape, 1)
    before = jnp.where(row < data, 0.0, 1.0)
    stride = 1
    while True:
        up = (me & stride) != 0
        mine, theirs = total[:, data : data + 1], decay_in(got, data)
        other = got.astype(F)
        if stride > 1:
            lead = before[:, data : data + 1]
            before = jnp.where(
                up, jnp.where(row < data, lead * other + before, lead * theirs), before
            )
        if stride * 2 >= shards:
            break
        total = jnp.where(
            row < data,
            jnp.where(up, 1.0, theirs) * total + jnp.where(up, mine, 1.0) * other,
            mine * theirs,
        )
        stride *= 2
        moves = [(i, i ^ stride) for i in range(shards)]
        if stride * 2 >= shards:
            moves = [m for m in moves if m[0] < m[1]]
        pay = payload(total, data)
        got = lax.ppermute(pay, "seq", moves)
        late = yield pay
        got = after(got, *late)
    theirs = lax.ppermute(before, "seq", [(i, i ^ 1) for i in range(shards)])
    late = yield before
    theirs = after(theirs, *late)
    yield before, theirs, first


class Run:
    def __init__(self, steps):
        self.steps = steps
        self.sent = next(steps)
        self.state = None

    def step(self, *late):
        out = self.steps.send(late)
        if isinstance(out, tuple):
            self.state = out
        else:
            self.sent = out
        return self

    def finish(self, *late):
        while self.state is None:
            self.step(*late)
            late = ()
        return self.state


def state_of(c, j, data, mine, theirs, first, start):
    half, _, width = mine.shape
    at = j % half
    same = c == j // half
    body = data // 16 * 16
    before = jnp.where(same, mine[at], theirs[at])
    tail = first[j, body:].astype(F)
    off = data - body
    decay = jnp.where(
        c == 0, 1.0, tail[off : off + 1] + tail[off + 1 : off + 2] + tail[off + 2 : off + 3]
    )
    scale = jnp.where(c == 0, 0.0, 1.0)
    rows = decay * before[:body] + scale * first[j, :body].astype(F)
    if off:
        diagonal = decay * before[body : body + 1] + scale * tail[:1]
        rows = unpack(rows, diagonal)
    return rows + (decay * before[data : data + 1]) * start[j]


def weights_kernel(chunk, width, count, queries, run, square, weight_out, query_out, wide):
    tokens = queries.shape[0]
    at = lax.broadcasted_iota(jnp.int32, (1, tokens), 1)
    now = run[...]
    wide[...] = jnp.zeros_like(wide)
    wide[:chunk] = jnp.where(at < count[0], now + jnp.log(square[...]), DEAD)
    tall = wide[...].T
    row = lax.broadcasted_iota(jnp.int32, (tokens, tokens), 0)
    col = lax.broadcasted_iota(jnp.int32, (tokens, tokens), 1)
    for j in range(chunk):
        weight_out[j] = jnp.where(row <= col, jnp.exp(now[j : j + 1] - tall[:, j : j + 1]), 0.0)
        q = queries[:, j * width : (j + 1) * width].astype(F).T
        query_out[j] = q * lax.rsqrt(jnp.sum(q * q, axis=0, keepdims=True) + 1e-06)


def weights_call(count, queries, run, square, width, place):
    tokens = queries.shape[0]
    chunk = run.shape[0]
    shapes = [
        jax.ShapeDtypeStruct((chunk, tokens, tokens), F),
        jax.ShapeDtypeStruct((chunk, width, tokens), F),
    ]
    return pl.pallas_call(
        functools.partial(weights_kernel, chunk, width),
        grid=(1,),
        in_specs=[
            SMEM,
            spec((tokens, chunk * width), lambda i: (0, place)),
            whole(run.shape),
            whole(square.shape),
        ],
        out_specs=[whole(s.shape) for s in shapes],
        out_shape=shapes,
        scratch_shapes=[pltpu.VMEM((128, tokens), F)],
        compiler_params=params(20),
        cost_estimate=cost(3),
        name="weights",
    )(count, queries, run, square)


def solve_kernel(
    chunk, width, opening, side, keys, keyt, queries, weights, run, ridge_rows, *rest
):
    tokens = keys.shape[0]
    half_t = tokens // 2
    c = side[0]
    if opening:
        mine, theirs, first, start, answer_out, left, dirs, resid, norm_out, *rest = rest
    else:
        answer_in, left, dirs_in, resid_in, norm_in, answer_out, dirs, resid, *rest = rest
    near_top, near_low, far, ridge = rest
    lead = []
    norms = []
    for j in range(chunk):
        ridge[j] = jnp.broadcast_to(ridge_rows[j : j + 1], (width, width)).T
        lead.append(jnp.exp(run[j : j + 1, :]))
        if not opening:
            dirs[j] = dirs_in[j]
            resid[j] = resid_in[j]
            answer_out[j] = answer_in[j]
            norms.append(norm_in[j : j + 1, :])
            continue
        key = keys[:, j * width : (j + 1) * width]
        left[j, :tokens, :width] = key
        left[j, :tokens, width:] = key
        gram = state_of(c, j, width // 2 + 1, mine, theirs, first, start).astype(B)
        left[j, tokens:, :width] = gram
        left[j, tokens:, width:] = gram
        q = queries[j]
        dirs[j] = q
        resid[j] = q
        answer_out[j] = jnp.zeros_like(q)
        norms.append(jnp.sum(q * q, axis=0, keepdims=True))

    def spread(j, fine):
        p = dirs[j]
        if fine:
            hi, lo = split(p)
            image = dot(left[j], jnp.concatenate([hi, lo], 0))
        else:
            image = dot(left[j, :, :width], p.astype(B))
        far[j] = image[tokens:]
        top = image[:half_t] * weights[j, :half_t]
        low = image[half_t:tokens, half_t:] * weights[j, half_t:, half_t:]
        if fine:
            near_top[j, 0], near_top[j, 1] = split(top)
            near_low[j, 0], near_low[j, 1] = split(low)
        else:
            near_top[j, 0] = top.astype(B)
            near_low[j, 0] = low.astype(B)

    def gather(j, fine, norm):
        kt = keyt[j]
        p = dirs[j]
        if fine:
            early = kt[:, :half_t]
            one = dot(
                jnp.concatenate([early, early], 1),
                jnp.concatenate([near_top[j, 0, :, :half_t], near_top[j, 1, :, :half_t]], 0),
            )
            two = dot(
                kt,
                jnp.concatenate(
                    [
                        jnp.concatenate([near_top[j, 0, :, half_t:], near_top[j, 1, :, half_t:]], 1),
                        jnp.concatenate([near_low[j, 0], near_low[j, 1]], 1),
                    ],
                    0,
                ),
            )
            near = jnp.concatenate([one, two[:, :half_t] + two[:, half_t:]], 1)
        else:
            low = near_low[j, 0]
            near = dot(
                kt,
                jnp.concatenate(
                    [near_top[j, 0], jnp.concatenate([jnp.zeros_like(low), low], 1)], 0
                ),
            )
        image = lead[j] * far[j] + near + jnp.concatenate([ridge[j]] * (tokens // width), 1) * p
        step = norm / jnp.sum(p * image, axis=0, keepdims=True)
        answer_out[j] = answer_out[j] + step * p
        r = resid[j] - step * image
        resid[j] = r
        after = jnp.sum(r * r, axis=0, keepdims=True)
        dirs[j] = r + (after / norm) * p
        return after

    cut = max(chunk // 2, 1)
    pairs = list(zip(range(cut), range(cut, chunk)))

    def turn(fine, more):
        def body(_, norms):
            norms = list(norms)
            for a, b in pairs:
                spread(b, fine)
                norms[a] = gather(a, fine, norms[a])
            for a, b in pairs:
                if more:
                    spread(a, fine)
                norms[b] = gather(b, fine, norms[b])
            return tuple(norms)

        return body

    for a, _ in pairs:
        spread(a, opening)
    turns = FINE if opening else ITERS - FINE
    norms = lax.fori_loop(0, turns - 1, turn(opening, True), tuple(norms))
    norms = turn(opening, False)(0, norms)
    if opening:
        for j in range(chunk):
            norm_out[j : j + 1, :] = norms[j]


def solve_call(side, keys, keyt, queries, weights, run, ridge, rest, start, place):
    opening = start is not None
    tokens = keys.shape[0]
    chunk, width, _ = keyt.shape
    block = spec((tokens, chunk * width), lambda i: (0, place))
    ins = [side, keys, keyt, queries, weights, run, ridge, *rest]
    in_specs = (
        [SMEM, block]
        + [whole(a.shape) for a in ins[2:6]]
        + [spec((chunk, width), lambda i: (place, 0))]
        + [whole(a.shape) for a in rest]
    )
    columns = jax.ShapeDtypeStruct((chunk, width, tokens), F)
    state = pltpu.VMEM((chunk, width, tokens), F)
    if opening:
        ins.append(start)
        in_specs.append(spec((chunk, width, width), lambda i: (place, 0, 0)))
        shapes = [
            columns,
            jax.ShapeDtypeStruct((chunk, tokens + width, 2 * width), B),
            columns,
            columns,
            jax.ShapeDtypeStruct((chunk, tokens), F),
        ]
        scratch = []
    else:
        shapes = [columns]
        scratch = [state, state]
    return pl.pallas_call(
        functools.partial(solve_kernel, chunk, width, opening),
        grid=(1,),
        in_specs=in_specs,
        out_specs=[whole(s.shape) for s in shapes],
        out_shape=shapes,
        scratch_shapes=scratch
        + [
            pltpu.VMEM((chunk, 2, tokens // 2, tokens), B),
            pltpu.VMEM((chunk, 2, tokens // 2, tokens // 2), B),
            state,
            pltpu.VMEM((chunk, width, width), F),
        ],
        compiler_params=params(30),
        cost_estimate=cost(11 if opening else 9),
        name="solve_fine" if opening else "solve",
    )(*ins)


def readout_kernel(
    chunk, width, batch, side, keys, values, answers, weights, run, square, gain,
    mine, theirs, first, start, out_weight, count, into, out, total, state,
):
    tokens = keys.shape[0]
    i = pl.program_id(0)
    c = side[0]

    @pl.when(i == 0)
    def _():
        for j in range(chunk):
            state[j] = state_of(c, j, width, mine, theirs, first, start).astype(B)
        total[...] = jnp.zeros_like(total) if into is None else into[...]

    at = lax.broadcasted_iota(jnp.int32, (1, tokens), 1)
    live = (at < count[0]).astype(F)
    rows = []
    for j in range(batch):
        cols = slice(j * width, (j + 1) * width)
        line = pl.ds(i * batch + j, 1)
        hi, lo = split(answers[j])
        both = jnp.concatenate([hi, lo], 0)
        key = keys[:, cols]
        near = (dot(jnp.concatenate([key, key], 1), both) * weights[j]).astype(B)
        value = (values[:, cols].astype(F).T * jnp.sqrt(square[line, :])).astype(B)
        memory = state[i * batch + j]
        o = jnp.exp(run[line, :]) * dot(jnp.concatenate([memory, memory], 1), both) + dot(value, near)
        scale = lax.rsqrt(jnp.mean(o * o, axis=0, keepdims=True) + 1e-05) * live
        rows.append((o * scale).T * gain[:, cols])
    y = jnp.concatenate(rows, 1).astype(B)
    total[...] += dot(y, out_weight[...])

    @pl.when(i == pl.num_programs(0) - 1)
    def _():
        out[...] = total[...].astype(out.dtype)


def readout_call(
    side, keys, values, answers, weights, run, square, gain, state, start, out_weight, count, into, place, last
):
    tokens = keys.shape[0]
    chunk, width, _ = answers.shape
    model = out_weight.shape[1]
    batch = min(chunk, BATCH)
    turns = chunk // batch
    base = place * turns
    tok = spec((tokens, batch * width), lambda i: (0, base + i))
    ins = [side, keys, values, answers, weights, run, square, gain.reshape(1, -1), *state, start,
           out_weight, count]
    in_specs = [
        SMEM,
        tok,
        tok,
        spec((batch, width, tokens), lambda i: (i, 0, 0)),
        spec((batch, tokens, tokens), lambda i: (i, 0, 0)),
        whole(run.shape),
        whole(square.shape),
        spec((1, batch * width), lambda i: (0, base + i)),
        *[whole(a.shape) for a in state],
        spec((chunk, width, width), lambda i: (place, 0, 0)),
        spec((batch * width, model), lambda i: (base + i, 0)),
        SMEM,
    ]
    if into is not None:
        ins.append(into)
        in_specs.append(whole(into.shape))

    def body(*refs):
        refs = list(refs)
        if into is None:
            refs.insert(14, None)
        readout_kernel(chunk, width, batch, *refs)

    return pl.pallas_call(
        body,
        grid=(turns,),
        in_specs=in_specs,
        out_specs=whole((tokens, model)),
        out_shape=jax.ShapeDtypeStruct((tokens, model), B if last else F),
        scratch_shapes=[
            pltpu.VMEM((tokens, model), F),
            pltpu.VMEM((chunk, width, width), B),
        ],
        compiler_params=params(26),
        cost_estimate=cost(8),
        name="readout",
    )(*ins)


def local(
    shards, columns,
    queries, key_vectors, value_vectors, forget_gates, shard_counts, gram_start,
    memory_start, ridge_terms, norm_gain, out_weight,
):
    heads = forget_gates.shape[1]
    width = queries.shape[1] // heads
    chunk = min(heads, 8)
    parts = range(heads // chunk)
    side = jnp.stack([lax.axis_index("seq").astype(jnp.int32) & 1])
    gates = forget_gates.T
    grams = [gram_call(shard_counts, gates, key_vectors, chunk, n) for n in parts]
    runs = [grams[n][3] for n in parts]
    squares = [grams[n][4] for n in parts]

    gram_runs = [Run(prefix(g[0], g[1], width // 2 + 1, shards)) for g in grams]
    for r in gram_runs:
        r.step()
    values = after(value_vectors, *[r.sent for r in gram_runs])
    memories = [
        memory_call(shard_counts, runs[n], squares[n], key_vectors, values, width, n)
        for n in parts
    ]
    memory_runs = [Run(prefix(m[0], m[1], width, shards)) for m in memories]
    for r in gram_runs:
        r.step(*[m.sent for m in memory_runs])
    held = after(queries, *[r.sent for r in gram_runs])
    weights = [weights_call(shard_counts, held, runs[n], squares[n], width, n) for n in parts]
    for r in gram_runs:
        r.step()
    for m in memory_runs:
        m.step(*[r.sent for r in gram_runs])
    gram_states = [r.finish() for r in gram_runs]

    answers = []
    for n in parts:
        common = (side, key_vectors, grams[n][2])
        more = (weights[n][0], runs[n], ridge_terms)
        vectors = after(weights[n][1], *[m.sent for m in memory_runs])
        found = list(solve_call(*common, vectors, *more, gram_states[n], gram_start, n))
        for m in memory_runs:
            if m.state is None:
                m.step(found[0])
        found[0] = after(found[0], *[m.sent for m in memory_runs])
        found = solve_call(*common, vectors, *more, found, None, n)
        if n < len(parts) - 1:
            for m in memory_runs:
                if m.state is None:
                    m.step(found[0])
        answers.append(found[0])
    memory_states = [m.finish(answers[-1]) for m in memory_runs]
    mixed = None
    for n in parts:
        mixed = readout_call(
            side, key_vectors, value_vectors, answers[n], weights[n][0], runs[n], squares[n],
            norm_gain, memory_states[n], memory_start, out_weight, shard_counts, mixed, n,
            n == len(parts) - 1,
        )
    if columns > 1:
        mixed = lax.psum_scatter(mixed, "head", scatter_dimension=1, tiled=True)
    return mixed


def solution(mesh):
    return jax.shard_map(
        functools.partial(local, mesh.shape["seq"], mesh.shape["head"]),
        mesh=mesh,
        in_specs=(
            P("seq", "head"),
            P("seq", "head"),
            P("seq", "head"),
            P("seq", "head"),
            P("seq"),
            P("head", None, None),
            P("head", None, None),
            P("head", None),
            P("head"),
            P("head", None),
        ),
        out_specs=P("seq", "head"),
        check_vma=False,
    )
```

```python
import functools

import jax
import jax.numpy as jnp
from jax import lax
from jax.experimental import pallas as pl
from jax.experimental.pallas import tpu as pltpu
from jax.sharding import PartitionSpec as P

ITERS = 16
FINE = 9
BATCH = 4
F = jnp.float32
B = jnp.bfloat16
DEAD = 1e30
MIB = 1 << 20


def split(a):
    hi = a.astype(B)
    return hi, (a - hi.astype(F)).astype(B)


def dot(a, b):
    return jnp.dot(a, b, preferred_element_type=F)


def spec(block, index):
    return pl.BlockSpec(block, index)


def whole(shape):
    zeros = (0,) * len(shape)
    return pl.BlockSpec(shape, lambda *_: zeros)


SMEM = pl.BlockSpec(memory_space=pltpu.SMEM)


def params(mib):
    return pltpu.CompilerParams(vmem_limit_bytes=mib * MIB)


def cost(us):
    return pl.CostEstimate(flops=int(us * 1e9), bytes_accessed=int(us * 1e6), transcendentals=0)


def split_rows(tail, decay, lead):
    first = decay.astype(B).astype(F)
    second = (decay - first).astype(B).astype(F)
    third = decay - first - second
    row = lax.broadcasted_iota(jnp.int32, tail, 0)
    n = 0
    out = jnp.zeros(tail, F)
    if lead is not None:
        out = jnp.where(row == 0, lead, out)
        n = 1
    for value in (first, second, third):
        out = jnp.where(row == n, value, out)
        n += 1
    return out.astype(B)


def emit(sums_out, pay_out, j, body, decay, lead):
    height = body.shape[0]
    width = body.shape[1]
    sums_out[j, :height] = body
    row = lax.broadcasted_iota(jnp.int32, (16, width), 0)
    wide = jnp.broadcast_to(decay, (16, width))
    sums_out[j, height:] = wide if lead is None else jnp.where(row == 0, lead, wide)
    if pay_out is not None:
        pay_out[j, :height] = body.astype(B)
        pay_out[j, height:] = split_rows((16, width), wide, lead)


def pack(gram):
    half = gram.shape[0] // 2
    turned = pltpu.roll(gram[half:], half, 1)
    row = lax.broadcasted_iota(jnp.int32, turned.shape, 0)
    col = lax.broadcasted_iota(jnp.int32, turned.shape, 1)
    body = jnp.where((col < half) & (row < col), turned, gram[:half])
    diagonal = jnp.sum(jnp.where(row == col, turned, 0.0), axis=0, keepdims=True)
    return body, diagonal


def unpack(body, diagonal):
    half, width = body.shape
    flipped = jnp.concatenate([body, jnp.zeros_like(body)], 0).T
    row = lax.broadcasted_iota(jnp.int32, body.shape, 0)
    col = lax.broadcasted_iota(jnp.int32, body.shape, 1)
    top = jnp.where((col < half) & (row < col), flipped[:half], body)
    corner = jnp.where(row < col, body, jnp.where(row == col, diagonal, flipped[:half]))
    low = jnp.where(col < half, flipped[half:], pltpu.roll(corner, half, 1))
    return jnp.concatenate([top, low], 0)


def gram_kernel(chunk, width, count, gates, keys, sums_out, pay_out, run_out, square_out):
    tokens = keys.shape[0]
    at = lax.broadcasted_iota(jnp.int32, (1, tokens), 1)
    live = at < count[0]
    row = lax.broadcasted_iota(jnp.int32, (tokens, tokens), 0)
    col = lax.broadcasted_iota(jnp.int32, (tokens, tokens), 1)
    run = jnp.dot(
        jnp.where(live, jnp.log(gates[...]), 0.0),
        (row <= col).astype(F),
        preferred_element_type=F,
        precision=lax.Precision.HIGHEST,
    )
    run_out[...] = run
    for j in range(chunk):
        key = keys[:, j * width : (j + 1) * width]
        keyt = key.astype(F).T
        square = jnp.sum(keyt * keyt, axis=0, keepdims=True) + 1e-06
        now = run[j : j + 1]
        last = now[:, tokens - 1 :]
        tail = jnp.where(live, jnp.exp(last - now), 0.0)
        square_out[j : j + 1, :] = square
        hi, lo = split(keyt * (tail / square))
        gram = dot(jnp.concatenate([hi, lo], 1), jnp.concatenate([key, key], 0))
        body, diagonal = pack(gram)
        emit(sums_out, pay_out, j, body, jnp.broadcast_to(jnp.exp(last), (1, width)), diagonal)


def stack(a, chunk):
    block = (chunk, *a.shape[1:])
    zeros = (0,) * (len(block) - 1)
    return pl.BlockSpec(block, lambda i: (i, *zeros))


def gram_call(count, gates, keys, chunk):
    tokens = keys.shape[0]
    heads = gates.shape[0]
    width = keys.shape[1] // heads
    rows = width // 2 + 16
    shapes = [
        jax.ShapeDtypeStruct((heads, rows, width), F),
        jax.ShapeDtypeStruct((heads, rows, width), B),
        jax.ShapeDtypeStruct((heads, tokens), F),
        jax.ShapeDtypeStruct((heads, tokens), F),
    ]
    return pl.pallas_call(
        functools.partial(gram_kernel, chunk, width),
        grid=(heads // chunk,),
        in_specs=[
            SMEM,
            spec((chunk, tokens), lambda i: (i, 0)),
            spec((tokens, chunk * width), lambda i: (0, i)),
        ],
        out_specs=[stack(s, chunk) for s in shapes],
        out_shape=shapes,
        compiler_params=params(16),
        cost_estimate=cost(3),
        name="gram_sums",
    )(count, gates, keys)


def memory_kernel(chunk, width, count, run, square, keys, values, sums_out, pay_out):
    tokens = keys.shape[0]
    at = lax.broadcasted_iota(jnp.int32, (1, tokens), 1)
    live = at < count[0]
    for j in range(chunk):
        cols = slice(j * width, (j + 1) * width)
        key = keys[:, cols]
        now = run[j : j + 1]
        last = now[:, tokens - 1 :]
        tail = jnp.where(live, jnp.exp(last - now), 0.0)
        hi, lo = split(values[:, cols].astype(F).T * (tail * lax.rsqrt(square[j : j + 1])))
        memory = dot(jnp.concatenate([hi, lo], 1), jnp.concatenate([key, key], 0))
        emit(sums_out, pay_out, j, memory, jnp.broadcast_to(jnp.exp(last), (1, width)), None)


def memory_call(count, run, square, keys, values, width, chunk):
    tokens = keys.shape[0]
    heads = run.shape[0]
    block = spec((tokens, chunk * width), lambda i: (0, i))
    shapes = [
        jax.ShapeDtypeStruct((heads, width + 16, width), F),
        jax.ShapeDtypeStruct((heads, width + 16, width), B),
    ]
    return pl.pallas_call(
        functools.partial(memory_kernel, chunk, width),
        grid=(heads // chunk,),
        in_specs=[SMEM, stack(run, chunk), stack(square, chunk), block, block],
        out_specs=[stack(s, chunk) for s in shapes],
        out_shape=shapes,
        compiler_params=params(16),
        cost_estimate=cost(2),
        name="memory_sums",
    )(count, run, square, keys, values)


def decay_of(tail, off):
    return tail[off : off + 1] + tail[off + 1 : off + 2] + tail[off + 2 : off + 3]


def fold_kernel(half, data, bit, final, me, total, got, *rest):
    width = total.shape[2]
    body = data // 16 * 16
    off = data - body
    side = me[0] & 1
    up = ((me[0] >> bit) & 1) == 1
    rest = list(rest)
    before = rest.pop(0) if bit > 1 else None
    for j in range(half):
        at = side * half + j if bit == 0 else j
        tail = got[at, body:].astype(F)
        theirs = decay_of(tail, off)
        mine = total[at, data : data + 1]
        other = got[at, :body].astype(F)
        if not final:
            keep = jnp.where(up, 1.0, theirs)
            take = jnp.where(up, mine, 1.0)
            lead = keep * total[at, body : body + 1] + take * tail[:1] if off else None
            emit(
                rest[0], rest[1], j, keep * total[at, :body] + take * other, mine * theirs, lead
            )
        if bit > 0:
            gate = jnp.where(up, 1.0, 0.0)
            if before is None:
                inner, lead, decay = gate * other, gate * tail[:1], jnp.where(up, theirs, 1.0)
            else:
                scale = gate * before[j, data : data + 1]
                inner = scale * other + before[j, :body]
                lead = scale * tail[:1] + before[j, body : body + 1]
                decay = before[j, data : data + 1] * jnp.where(up, theirs, 1.0)
            emit(rest[-1], None, j, inner, decay, lead if off else None)


def fold(me, total, got, before, data, bit, final):
    half = got.shape[0] // 2 if bit == 0 else got.shape[0]
    _, rows, width = total.shape
    sums = jax.ShapeDtypeStruct((half, rows, width), F)
    ins = [me, total, got] + ([] if before is None else [before])
    shapes = ([] if final else [sums, jax.ShapeDtypeStruct((half, rows, width), B)]) + (
        [] if bit == 0 else [sums]
    )
    return pl.pallas_call(
        functools.partial(fold_kernel, half, data, bit, final),
        in_specs=[SMEM] + [whole(a.shape) for a in ins[1:]],
        out_specs=[whole(s.shape) for s in shapes],
        out_shape=shapes,
        compiler_params=params(16),
        cost_estimate=cost(1),
        name="fold",
    )(*ins)


def after(a, *others):
    return lax.optimization_barrier((a, *others))[0]


def prefix(me, sums, pay, data, shards):
    first = lax.ppermute(pay, "seq", [(i, i ^ 1) for i in range(shards)])
    late = yield pay
    first = after(first, *late)
    total, got, before = sums, first, None
    bit = 0
    while True:
        final = 2 << bit >= shards
        outs = fold(me, total, got, before, data, bit, final)
        if bit > 0:
            before = outs[-1]
        if final:
            break
        total, pay = outs[:2]
        bit += 1
        stride = 1 << bit
        moves = [(i, i ^ stride) for i in range(shards)]
        if stride * 2 >= shards:
            moves = [m for m in moves if m[0] < m[1]]
        got = lax.ppermute(pay, "seq", moves)
        late = yield pay
        got = after(got, *late)
    theirs = lax.ppermute(before, "seq", [(i, i ^ 1) for i in range(shards)])
    late = yield before
    theirs = after(theirs, *late)
    yield before, theirs, first


class Run:
    def __init__(self, steps):
        self.steps = steps
        self.sent = next(steps)
        self.state = None

    def step(self, *late):
        out = self.steps.send(late)
        if isinstance(out, tuple):
            self.state = out
        else:
            self.sent = out
        return self

    def finish(self, *late):
        while self.state is None:
            self.step(*late)
            late = ()
        return self.state


def state_of(c, head, data, mine, theirs, first, start):
    half = mine.shape[0]
    at = lax.rem(jnp.int32(head), jnp.int32(half))
    same = c == lax.div(jnp.int32(head), jnp.int32(half))
    body = data // 16 * 16
    off = data - body
    before = jnp.where(same, mine[at], theirs[at])
    tail = first[head, body:].astype(F)
    decay = jnp.where(c == 0, 1.0, decay_of(tail, off))
    scale = jnp.where(c == 0, 0.0, 1.0)
    rows = decay * before[:body] + scale * first[head, :body].astype(F)
    if off:
        diagonal = decay * before[body : body + 1] + scale * tail[:1]
        rows = unpack(rows, diagonal)
    return rows + (decay * before[data : data + 1]) * start


def weights_kernel(
    chunk, width, count, keys, queries, run, square, weight_out, query_out, keyt_out, wide
):
    tokens = queries.shape[0]
    at = lax.broadcasted_iota(jnp.int32, (1, tokens), 1)
    now = run[...]
    wide[...] = jnp.zeros_like(wide)
    wide[:chunk] = jnp.where(at < count[0], now + jnp.log(square[...]), DEAD)
    tall = wide[...].T
    row = lax.broadcasted_iota(jnp.int32, (tokens, tokens), 0)
    col = lax.broadcasted_iota(jnp.int32, (tokens, tokens), 1)
    for j in range(chunk):
        weight_out[j] = jnp.where(row <= col, jnp.exp(now[j : j + 1] - tall[:, j : j + 1]), 0.0)
        cols = slice(j * width, (j + 1) * width)
        keyt_out[j] = keys[:, cols].T
        q = queries[:, cols].astype(F).T
        query_out[j] = q * lax.rsqrt(jnp.sum(q * q, axis=0, keepdims=True) + 1e-06)


def weights_call(count, keys, queries, run, square, width, chunk):
    tokens = queries.shape[0]
    heads = run.shape[0]
    shapes = [
        jax.ShapeDtypeStruct((heads, tokens, tokens), F),
        jax.ShapeDtypeStruct((heads, width, tokens), F),
        jax.ShapeDtypeStruct((heads, width, tokens), B),
    ]
    block = spec((tokens, chunk * width), lambda i: (0, i))
    return pl.pallas_call(
        functools.partial(weights_kernel, chunk, width),
        grid=(heads // chunk,),
        in_specs=[
            SMEM,
            block,
            block,
            stack(run, chunk),
            stack(square, chunk),
        ],
        out_specs=[stack(s, chunk) for s in shapes],
        out_shape=shapes,
        scratch_shapes=[pltpu.VMEM((128, tokens), F)],
        compiler_params=params(20),
        cost_estimate=cost(2),
        name="weights",
    )(count, keys, queries, run, square)


def solve_kernel(
    chunk, width, base, opening, me, keys, keyt, queries, weights, run, ridge_rows, *rest
):
    tokens = keys.shape[0]
    half_t = tokens // 2
    c = me[0] & 1
    if opening:
        mine, theirs, first, start, answer_out, left, dirs, resid, norm_out, *rest = rest
    else:
        answer_in, left, dirs_in, resid_in, norm_in, answer_out, dirs, resid, *rest = rest
    near_top, near_low, far, ridge = rest
    lead = []
    norms = []
    for j in range(chunk):
        ridge[j] = jnp.broadcast_to(ridge_rows[j : j + 1], (width, width)).T
        lead.append(jnp.exp(run[j : j + 1, :]))
        if not opening:
            dirs[j] = dirs_in[j]
            resid[j] = resid_in[j]
            answer_out[j] = answer_in[j]
            norms.append(norm_in[j : j + 1, :])
            continue
        key = keys[:, j * width : (j + 1) * width]
        left[j, :tokens, :width] = key
        left[j, :tokens, width:] = key
        gram = state_of(c, base + j, width // 2 + 1, mine, theirs, first, start[j]).astype(B)
        left[j, tokens:, :width] = gram
        left[j, tokens:, width:] = gram
        q = queries[j]
        dirs[j] = q
        resid[j] = q
        answer_out[j] = jnp.zeros_like(q)
        norms.append(jnp.sum(q * q, axis=0, keepdims=True))

    def spread(j, fine):
        p = dirs[j]
        if fine:
            hi, lo = split(p)
            image = dot(left[j], jnp.concatenate([hi, lo], 0))
        else:
            image = dot(left[j, :, :width], p.astype(B))
        far[j] = image[tokens:]
        top = image[:half_t] * weights[j, :half_t]
        low = image[half_t:tokens, half_t:] * weights[j, half_t:, half_t:]
        if fine:
            near_top[j, 0], near_top[j, 1] = split(top)
            near_low[j, 0], near_low[j, 1] = split(low)
        else:
            near_top[j, 0] = top.astype(B)
            near_low[j, 0] = low.astype(B)

    def gather(j, fine, norm):
        kt = keyt[j]
        p = dirs[j]
        if fine:
            early = kt[:, :half_t]
            one = dot(
                jnp.concatenate([early, early], 1),
                jnp.concatenate([near_top[j, 0, :, :half_t], near_top[j, 1, :, :half_t]], 0),
            )
            two = dot(
                kt,
                jnp.concatenate(
                    [
                        jnp.concatenate([near_top[j, 0, :, half_t:], near_top[j, 1, :, half_t:]], 1),
                        jnp.concatenate([near_low[j, 0], near_low[j, 1]], 1),
                    ],
                    0,
                ),
            )
            near = jnp.concatenate([one, two[:, :half_t] + two[:, half_t:]], 1)
        else:
            low = near_low[j, 0]
            near = dot(
                kt,
                jnp.concatenate(
                    [near_top[j, 0], jnp.concatenate([jnp.zeros_like(low), low], 1)], 0
                ),
            )
        image = lead[j] * far[j] + near + jnp.concatenate([ridge[j]] * (tokens // width), 1) * p
        step = norm / jnp.sum(p * image, axis=0, keepdims=True)
        answer_out[j] = answer_out[j] + step * p
        r = resid[j] - step * image
        resid[j] = r
        after = jnp.sum(r * r, axis=0, keepdims=True)
        dirs[j] = r + (after / norm) * p
        return after

    cut = max(chunk // 2, 1)
    pairs = list(zip(range(cut), range(cut, chunk)))

    def turn(fine, more):
        def body(_, norms):
            norms = list(norms)
            for a, b in pairs:
                spread(b, fine)
                norms[a] = gather(a, fine, norms[a])
            for a, b in pairs:
                if more:
                    spread(a, fine)
                norms[b] = gather(b, fine, norms[b])
            return tuple(norms)

        return body

    for a, _ in pairs:
        spread(a, opening)
    turns = FINE if opening else ITERS - FINE
    norms = lax.fori_loop(0, turns - 1, turn(opening, True), tuple(norms))
    norms = turn(opening, False)(0, norms)
    if opening:
        for j in range(chunk):
            norm_out[j : j + 1, :] = norms[j]


def solve_call(me, keys, keyt, queries, weights, run, ridge, rest, start, chunk, place):
    opening = start is not None
    tokens = keys.shape[0]
    width = keyt.shape[1]

    def mine(a):
        zeros = (0,) * (a.ndim - 1)
        return spec((chunk, *a.shape[1:]), lambda i: (place, *zeros))

    block = spec((tokens, chunk * width), lambda i: (0, place))
    ins = [me, keys, keyt, queries, weights, run, ridge, *rest]
    in_specs = (
        [SMEM, block]
        + [mine(a) for a in ins[2:7]]
        + [whole(a.shape) for a in rest]
    )
    columns = jax.ShapeDtypeStruct((chunk, width, tokens), F)
    state = pltpu.VMEM((chunk, width, tokens), F)
    if opening:
        ins.append(start)
        in_specs.append(spec((chunk, width, width), lambda i: (place, 0, 0)))
        shapes = [
            columns,
            jax.ShapeDtypeStruct((chunk, tokens + width, 2 * width), B),
            columns,
            columns,
            jax.ShapeDtypeStruct((chunk, tokens), F),
        ]
        scratch = []
    else:
        shapes = [columns]
        scratch = [state, state]
    return pl.pallas_call(
        functools.partial(solve_kernel, chunk, width, place * chunk, opening),
        grid=(1,),
        in_specs=in_specs,
        out_specs=[whole(s.shape) for s in shapes],
        out_shape=shapes,
        scratch_shapes=scratch
        + [
            pltpu.VMEM((chunk, 2, tokens // 2, tokens), B),
            pltpu.VMEM((chunk, 2, tokens // 2, tokens // 2), B),
            state,
            pltpu.VMEM((chunk, width, width), F),
        ],
        compiler_params=params(30),
        cost_estimate=cost(11 if opening else 9),
        name="solve_fine" if opening else "solve",
    )(*ins)


def readout_kernel(
    width, batch, parts, me, keys, values, weights, run, square, gain,
    mine, theirs, first, start, out_weight, count, *rest
):
    answers = rest[:parts]
    out, total = rest[parts:]
    tokens = keys.shape[0]
    i = pl.program_id(0)
    turns = pl.num_programs(0)
    c = me[0] & 1

    @pl.when(i == 0)
    def _():
        total[...] = jnp.zeros_like(total)

    at = lax.broadcasted_iota(jnp.int32, (1, tokens), 1)
    live = (at < count[0]).astype(F)
    rows = []
    for j in range(batch):
        cols = slice(j * width, (j + 1) * width)
        head = i * batch + j
        line = pl.ds(head, 1)
        answer = answers[0][j]
        for n in range(1, parts):
            answer = jnp.where(i * parts < n * turns, answer, answers[n][j])
        hi, lo = split(answer)
        both = jnp.concatenate([hi, lo], 0)
        key = keys[:, cols]
        near = (dot(jnp.concatenate([key, key], 1), both) * weights[j]).astype(B)
        value = (values[:, cols].astype(F).T * jnp.sqrt(square[line, :])).astype(B)
        memory = state_of(c, head, width, mine, theirs, first, start[j]).astype(B)
        o = jnp.exp(run[line, :]) * dot(jnp.concatenate([memory, memory], 1), both) + dot(value, near)
        scale = lax.rsqrt(jnp.mean(o * o, axis=0, keepdims=True) + 1e-05) * live
        rows.append((o * scale).T * gain[:, cols])
    y = jnp.concatenate(rows, 1).astype(B)
    total[...] += dot(y, out_weight[...])

    @pl.when(i == turns - 1)
    def _():
        out[...] = total[...].astype(B)


def readout_call(
    me, keys, values, answers, weights, run, square, gain, state, start, out_weight, count
):
    tokens = keys.shape[0]
    heads = run.shape[0]
    chunk, width, _ = answers[0].shape
    model = out_weight.shape[1]
    batch = min(chunk, BATCH)
    each = chunk // batch
    tok = spec((tokens, batch * width), lambda i: (0, i))
    ins = [me, keys, values, weights, run, square, gain.reshape(1, -1), *state, start,
           out_weight, count, *answers]

    def part(n):
        return spec(
            (batch, width, tokens), lambda i: (jnp.clip(i - n * each, 0, each - 1), 0, 0)
        )

    in_specs = [
        SMEM,
        tok,
        tok,
        stack(weights, batch),
        whole(run.shape),
        whole(square.shape),
        spec((1, batch * width), lambda i: (0, i)),
        *[whole(a.shape) for a in state],
        stack(start, batch),
        spec((batch * width, model), lambda i: (i, 0)),
        SMEM,
        *[part(n) for n in range(len(answers))],
    ]
    return pl.pallas_call(
        functools.partial(readout_kernel, width, batch, len(answers)),
        grid=(heads // batch,),
        in_specs=in_specs,
        out_specs=whole((tokens, model)),
        out_shape=jax.ShapeDtypeStruct((tokens, model), B),
        scratch_shapes=[pltpu.VMEM((tokens, model), F)],
        compiler_params=params(30),
        cost_estimate=cost(7),
        name="readout",
    )(*ins)


def local(
    shards, columns,
    queries, key_vectors, value_vectors, forget_gates, shard_counts, gram_start,
    memory_start, ridge_terms, norm_gain, out_weight,
):
    heads = forget_gates.shape[1]
    width = queries.shape[1] // heads
    chunk = min(heads, 8)
    parts = range(heads // chunk)
    me = lax.axis_index("seq").astype(jnp.int32).reshape(1)
    sums, pay, run, square = gram_call(shard_counts, forget_gates.T, key_vectors, chunk)

    gram = Run(prefix(me, sums, pay, width // 2 + 1, shards))
    gram.step()
    values = after(value_vectors, gram.sent)
    memory = Run(
        prefix(
            me,
            *memory_call(shard_counts, run, square, key_vectors, values, width, chunk),
            width,
            shards,
        )
    )
    gram.step(memory.sent)
    memory.step(gram.sent)
    weights, vectors, keyt = weights_call(
        shard_counts, key_vectors, after(queries, gram.sent, memory.sent), run, square, width, chunk
    )
    gram.step(vectors, memory.sent)
    if gram.state is None:
        gram.step()
    memory.step(gram.sent)
    if gram.state is None:
        gram.step(memory.sent)
    gram_state = gram.finish()

    answers = []
    last = memory.sent
    for n in parts:
        common = (weights, run, ridge_terms)
        opened = solve_call(
            me, key_vectors, keyt, after(vectors, last, memory.sent), *common,
            gram_state, gram_start, chunk, n,
        )
        opened = list(opened)
        if memory.state is None:
            memory.step(opened[0])
            opened[0] = after(opened[0], memory.sent)
        answers += solve_call(me, key_vectors, keyt, vectors, *common, opened, None, chunk, n)
        last = answers[-1]
        if n == 0 and memory.state is None:
            memory.step(last)
    memory_state = memory.finish(last)
    mixed = readout_call(
        me, key_vectors, value_vectors, answers, weights, run, square, norm_gain,
        memory_state, memory_start, out_weight, shard_counts,
    )
    if columns > 1:
        mixed = lax.psum_scatter(mixed, "head", scatter_dimension=1, tiled=True)
    return mixed


def solution(mesh):
    return jax.shard_map(
        functools.partial(local, mesh.shape["seq"], mesh.shape["head"]),
        mesh=mesh,
        in_specs=(
            P("seq", "head"),
            P("seq", "head"),
            P("seq", "head"),
            P("seq", "head"),
            P("seq"),
            P("head", None, None),
            P("head", None, None),
            P("head", None),
            P("head"),
            P("head", None),
        ),
        out_specs=P("seq", "head"),
        check_vma=False,
    )
```

```python
import functools

import jax
import jax.numpy as jnp
from jax import lax
from jax.experimental import pallas as pl
from jax.experimental.pallas import tpu as pltpu
from jax.sharding import PartitionSpec as P

ITERS = 16
FINE = 9
BATCH = 8
F = jnp.float32
B = jnp.bfloat16
DEAD = 1e30
MIB = 1 << 20


def split(a):
    hi = a.astype(B)
    return hi, (a - hi.astype(F)).astype(B)


def dot(a, b):
    return jnp.dot(a, b, preferred_element_type=F)


def spec(block, index):
    return pl.BlockSpec(block, index)


def whole(shape):
    zeros = (0,) * len(shape)
    return pl.BlockSpec(shape, lambda *_: zeros)


SMEM = pl.BlockSpec(memory_space=pltpu.SMEM)


def params(mib):
    return pltpu.CompilerParams(vmem_limit_bytes=mib * MIB)


def cost(us):
    return pl.CostEstimate(flops=int(us * 1e9), bytes_accessed=int(us * 1e6), transcendentals=0)


def split_rows(tail, decay, lead):
    first = decay.astype(B).astype(F)
    second = (decay - first).astype(B).astype(F)
    third = decay - first - second
    row = lax.broadcasted_iota(jnp.int32, tail, 0)
    n = 0
    out = jnp.zeros(tail, F)
    if lead is not None:
        out = jnp.where(row == 0, lead, out)
        n = 1
    for value in (first, second, third):
        out = jnp.where(row == n, value, out)
        n += 1
    return out.astype(B)


def emit(sums_out, pay_out, j, body, decay, lead):
    height = body.shape[0]
    width = body.shape[1]
    sums_out[j, :height] = body
    row = lax.broadcasted_iota(jnp.int32, (16, width), 0)
    wide = jnp.broadcast_to(decay, (16, width))
    sums_out[j, height:] = wide if lead is None else jnp.where(row == 0, lead, wide)
    if pay_out is not None:
        pay_out[j, :height] = body.astype(B)
        pay_out[j, height:] = split_rows((16, width), wide, lead)


def pack(gram):
    half = gram.shape[0] // 2
    turned = pltpu.roll(gram[half:], half, 1)
    row = lax.broadcasted_iota(jnp.int32, turned.shape, 0)
    col = lax.broadcasted_iota(jnp.int32, turned.shape, 1)
    body = jnp.where((col < half) & (row < col), turned, gram[:half])
    diagonal = jnp.sum(jnp.where(row == col, turned, 0.0), axis=0, keepdims=True)
    return body, diagonal


def unpack(body, diagonal):
    half, width = body.shape
    flipped = jnp.concatenate([body, jnp.zeros_like(body)], 0).T
    row = lax.broadcasted_iota(jnp.int32, body.shape, 0)
    col = lax.broadcasted_iota(jnp.int32, body.shape, 1)
    top = jnp.where((col < half) & (row < col), flipped[:half], body)
    corner = jnp.where(row < col, body, jnp.where(row == col, diagonal, flipped[:half]))
    low = jnp.where(col < half, flipped[half:], pltpu.roll(corner, half, 1))
    return jnp.concatenate([top, low], 0)


def gram_kernel(chunk, width, count, gates, keys, sums_out, pay_out, run_out, square_out):
    tokens = keys.shape[0]
    at = lax.broadcasted_iota(jnp.int32, (1, tokens), 1)
    live = at < count[0]
    row = lax.broadcasted_iota(jnp.int32, (tokens, tokens), 0)
    col = lax.broadcasted_iota(jnp.int32, (tokens, tokens), 1)
    run = jnp.dot(
        jnp.where(live, jnp.log(gates[...]), 0.0),
        (row <= col).astype(F),
        preferred_element_type=F,
        precision=lax.Precision.HIGHEST,
    )
    run_out[...] = run
    for j in range(chunk):
        key = keys[:, j * width : (j + 1) * width]
        keyt = key.astype(F).T
        square = jnp.sum(keyt * keyt, axis=0, keepdims=True) + 1e-06
        now = run[j : j + 1]
        last = now[:, tokens - 1 :]
        tail = jnp.where(live, jnp.exp(last - now), 0.0)
        square_out[j : j + 1, :] = square
        hi, lo = split(keyt * (tail / square))
        gram = dot(jnp.concatenate([hi, lo], 1), jnp.concatenate([key, key], 0))
        body, diagonal = pack(gram)
        emit(sums_out, pay_out, j, body, jnp.broadcast_to(jnp.exp(last), (1, width)), diagonal)


def stack(a, chunk):
    block = (chunk, *a.shape[1:])
    zeros = (0,) * (len(block) - 1)
    return pl.BlockSpec(block, lambda i: (i, *zeros))


def gram_call(count, gates, keys, chunk, place):
    tokens = keys.shape[0]
    heads = gates.shape[0]
    width = keys.shape[1] // heads
    rows = width // 2 + 16
    shapes = [
        jax.ShapeDtypeStruct((chunk, rows, width), F),
        jax.ShapeDtypeStruct((chunk, rows, width), B),
        jax.ShapeDtypeStruct((chunk, tokens), F),
        jax.ShapeDtypeStruct((chunk, tokens), F),
    ]
    return pl.pallas_call(
        functools.partial(gram_kernel, chunk, width),
        grid=(1,),
        in_specs=[
            SMEM,
            spec((chunk, tokens), lambda i: (place, 0)),
            spec((tokens, chunk * width), lambda i: (0, place)),
        ],
        out_specs=[stack(s, chunk) for s in shapes],
        out_shape=shapes,
        compiler_params=params(16),
        cost_estimate=cost(3),
        name="gram_sums",
    )(count, gates, keys)


def memory_kernel(chunk, width, count, run, square, keys, values, sums_out, pay_out):
    tokens = keys.shape[0]
    at = lax.broadcasted_iota(jnp.int32, (1, tokens), 1)
    live = at < count[0]
    for j in range(chunk):
        cols = slice(j * width, (j + 1) * width)
        key = keys[:, cols]
        now = run[j : j + 1]
        last = now[:, tokens - 1 :]
        tail = jnp.where(live, jnp.exp(last - now), 0.0)
        hi, lo = split(values[:, cols].astype(F).T * (tail * lax.rsqrt(square[j : j + 1])))
        memory = dot(jnp.concatenate([hi, lo], 1), jnp.concatenate([key, key], 0))
        emit(sums_out, pay_out, j, memory, jnp.broadcast_to(jnp.exp(last), (1, width)), None)


def memory_call(count, run, square, keys, values, width, chunk):
    tokens = keys.shape[0]
    heads = run.shape[0]
    block = spec((tokens, chunk * width), lambda i: (0, i))
    shapes = [
        jax.ShapeDtypeStruct((heads, width + 16, width), F),
        jax.ShapeDtypeStruct((heads, width + 16, width), B),
    ]
    return pl.pallas_call(
        functools.partial(memory_kernel, chunk, width),
        grid=(heads // chunk,),
        in_specs=[SMEM, stack(run, chunk), stack(square, chunk), block, block],
        out_specs=[stack(s, chunk) for s in shapes],
        out_shape=shapes,
        compiler_params=params(16),
        cost_estimate=cost(2),
        name="memory_sums",
    )(count, run, square, keys, values)


def decay_of(tail, off):
    return tail[off : off + 1] + tail[off + 1 : off + 2] + tail[off + 2 : off + 3]


def fold_kernel(half, data, bit, final, me, total, got, *rest):
    width = total.shape[2]
    body = data // 16 * 16
    off = data - body
    side = me[0] & 1
    up = ((me[0] >> bit) & 1) == 1
    rest = list(rest)
    before = rest.pop(0) if bit > 1 else None
    for j in range(half):
        at = side * half + j if bit == 0 else j
        tail = got[at, body:].astype(F)
        theirs = decay_of(tail, off)
        mine = total[at, data : data + 1]
        other = got[at, :body].astype(F)
        if not final:
            keep = jnp.where(up, 1.0, theirs)
            take = jnp.where(up, mine, 1.0)
            lead = keep * total[at, body : body + 1] + take * tail[:1] if off else None
            emit(
                rest[0], rest[1], j, keep * total[at, :body] + take * other, mine * theirs, lead
            )
        if bit > 0:
            gate = jnp.where(up, 1.0, 0.0)
            if before is None:
                inner, lead, decay = gate * other, gate * tail[:1], jnp.where(up, theirs, 1.0)
            else:
                scale = gate * before[j, data : data + 1]
                inner = scale * other + before[j, :body]
                lead = scale * tail[:1] + before[j, body : body + 1]
                decay = before[j, data : data + 1] * jnp.where(up, theirs, 1.0)
            emit(rest[-1], None, j, inner, decay, lead if off else None)


def fold(me, total, got, before, data, bit, final):
    half = got.shape[0] // 2 if bit == 0 else got.shape[0]
    _, rows, width = total.shape
    sums = jax.ShapeDtypeStruct((half, rows, width), F)
    ins = [me, total, got] + ([] if before is None else [before])
    shapes = ([] if final else [sums, jax.ShapeDtypeStruct((half, rows, width), B)]) + (
        [] if bit == 0 else [sums]
    )
    return pl.pallas_call(
        functools.partial(fold_kernel, half, data, bit, final),
        in_specs=[SMEM] + [whole(a.shape) for a in ins[1:]],
        out_specs=[whole(s.shape) for s in shapes],
        out_shape=shapes,
        compiler_params=params(16),
        cost_estimate=cost(1),
        name="fold",
    )(*ins)


def after(a, *others):
    return lax.optimization_barrier((a, *others))[0]


def prefix(me, sums, pay, data, shards):
    first = lax.ppermute(pay, "seq", [(i, i ^ 1) for i in range(shards)])
    late = yield pay
    first = after(first, *late)
    total, got, before = sums, first, None
    bit = 0
    while True:
        final = 2 << bit >= shards
        outs = fold(me, total, got, before, data, bit, final)
        if bit > 0:
            before = outs[-1]
        if final:
            break
        total, pay = outs[:2]
        bit += 1
        stride = 1 << bit
        moves = [(i, i ^ stride) for i in range(shards)]
        if stride * 2 >= shards:
            moves = [m for m in moves if m[0] < m[1]]
        got = lax.ppermute(pay, "seq", moves)
        late = yield pay
        got = after(got, *late)
    theirs = lax.ppermute(before, "seq", [(i, i ^ 1) for i in range(shards)])
    late = yield before
    theirs = after(theirs, *late)
    yield before, theirs, first


class Run:
    def __init__(self, steps):
        self.steps = steps
        self.sent = next(steps)
        self.state = None

    def step(self, *late):
        out = self.steps.send(late)
        if isinstance(out, tuple):
            self.state = out
        else:
            self.sent = out
        return self

    def finish(self, *late):
        while self.state is None:
            self.step(*late)
            late = ()
        return self.state


def state_of(c, head, data, mine, theirs, first, start):
    half = mine.shape[0]
    at = lax.rem(jnp.int32(head), jnp.int32(half))
    same = c == lax.div(jnp.int32(head), jnp.int32(half))
    body = data // 16 * 16
    off = data - body
    before = jnp.where(same, mine[at], theirs[at])
    tail = first[head, body:].astype(F)
    decay = jnp.where(c == 0, 1.0, decay_of(tail, off))
    scale = jnp.where(c == 0, 0.0, 1.0)
    rows = decay * before[:body] + scale * first[head, :body].astype(F)
    if off:
        diagonal = decay * before[body : body + 1] + scale * tail[:1]
        rows = unpack(rows, diagonal)
    return rows + (decay * before[data : data + 1]) * start


def weights_kernel(
    chunk, width, count, keys, queries, run, square, ridge, weight_out, query_out, keyt_out,
    ridge_out, wide,
):
    tokens = queries.shape[0]
    at = lax.broadcasted_iota(jnp.int32, (1, tokens), 1)
    now = run[...]
    wide[...] = jnp.zeros_like(wide)
    wide[:chunk] = jnp.where(at < count[0], now + jnp.log(square[...]), DEAD)
    tall = wide[...].T
    row = lax.broadcasted_iota(jnp.int32, (tokens, tokens), 0)
    col = lax.broadcasted_iota(jnp.int32, (tokens, tokens), 1)
    for j in range(chunk):
        weight_out[j] = jnp.where(row <= col, jnp.exp(now[j : j + 1] - tall[:, j : j + 1]), 0.0)
        cols = slice(j * width, (j + 1) * width)
        keyt_out[j] = keys[:, cols].T
        ridge_out[j] = jnp.broadcast_to(ridge[j : j + 1], (width, width)).T
        q = queries[:, cols].astype(F).T
        query_out[j] = q * lax.rsqrt(jnp.sum(q * q, axis=0, keepdims=True) + 1e-06)


def weights_call(count, keys, queries, run, square, ridge, width, chunk):
    tokens = queries.shape[0]
    heads = run.shape[0]
    shapes = [
        jax.ShapeDtypeStruct((heads, tokens, tokens), F),
        jax.ShapeDtypeStruct((heads, width, tokens), F),
        jax.ShapeDtypeStruct((heads, width, tokens), B),
        jax.ShapeDtypeStruct((heads, width, width), F),
    ]
    block = spec((tokens, chunk * width), lambda i: (0, i))
    return pl.pallas_call(
        functools.partial(weights_kernel, chunk, width),
        grid=(heads // chunk,),
        in_specs=[
            SMEM,
            block,
            block,
            stack(run, chunk),
            stack(square, chunk),
            stack(ridge, chunk),
        ],
        out_specs=[stack(s, chunk) for s in shapes],
        out_shape=shapes,
        scratch_shapes=[pltpu.VMEM((128, tokens), F)],
        compiler_params=params(20),
        cost_estimate=cost(2),
        name="weights",
    )(count, keys, queries, run, square, ridge)


def solve_kernel(
    chunk, width, base, opening, me, keys, keyt, queries, weights, run, ridge, *rest
):
    tokens = keys.shape[0]
    half_t = tokens // 2
    c = me[0] & 1
    if opening:
        mine, theirs, first, start, answer_out, left, dirs, resid, norm_out, *rest = rest
    else:
        answer_in, left, dirs_in, resid_in, norm_in, answer_out, dirs, resid, *rest = rest
    near_top, near_low, far = rest
    lead = []
    norms = []
    for j in range(chunk):
        lead.append(jnp.exp(run[j : j + 1, :]))
        if not opening:
            dirs[j] = dirs_in[j]
            resid[j] = resid_in[j]
            answer_out[j] = answer_in[j]
            norms.append(norm_in[j : j + 1, :])
            continue
        key = keys[:, j * width : (j + 1) * width]
        left[j, :tokens, :width] = key
        left[j, :tokens, width:] = key
        gram = state_of(c, base + j, width // 2 + 1, mine, theirs, first, start[j]).astype(B)
        left[j, tokens:, :width] = gram
        left[j, tokens:, width:] = gram
        q = queries[j]
        dirs[j] = q
        resid[j] = q
        answer_out[j] = jnp.zeros_like(q)
        norms.append(jnp.sum(q * q, axis=0, keepdims=True))

    def spread(j, fine):
        p = dirs[j]
        if fine:
            hi, lo = split(p)
            image = dot(left[j], jnp.concatenate([hi, lo], 0))
        else:
            image = dot(left[j, :, :width], p.astype(B))
        far[j] = image[tokens:]
        top = image[:half_t] * weights[j, :half_t]
        low = image[half_t:tokens, half_t:] * weights[j, half_t:, half_t:]
        if fine:
            near_top[j, 0], near_top[j, 1] = split(top)
            near_low[j, 0], near_low[j, 1] = split(low)
        else:
            near_top[j, 0] = top.astype(B)
            near_low[j, 0] = low.astype(B)

    def gather(j, fine, norm):
        kt = keyt[j]
        p = dirs[j]
        if fine:
            early = kt[:, :half_t]
            one = dot(
                jnp.concatenate([early, early], 1),
                jnp.concatenate([near_top[j, 0, :, :half_t], near_top[j, 1, :, :half_t]], 0),
            )
            two = dot(
                kt,
                jnp.concatenate(
                    [
                        jnp.concatenate([near_top[j, 0, :, half_t:], near_top[j, 1, :, half_t:]], 1),
                        jnp.concatenate([near_low[j, 0], near_low[j, 1]], 1),
                    ],
                    0,
                ),
            )
            near = jnp.concatenate([one, two[:, :half_t] + two[:, half_t:]], 1)
        else:
            low = near_low[j, 0]
            near = dot(
                kt,
                jnp.concatenate(
                    [near_top[j, 0], jnp.concatenate([jnp.zeros_like(low), low], 1)], 0
                ),
            )
        image = lead[j] * far[j] + near + jnp.concatenate([ridge[j]] * (tokens // width), 1) * p
        step = norm / jnp.sum(p * image, axis=0, keepdims=True)
        answer_out[j] = answer_out[j] + step * p
        r = resid[j] - step * image
        resid[j] = r
        after = jnp.sum(r * r, axis=0, keepdims=True)
        dirs[j] = r + (after / norm) * p
        return after

    cut = max(chunk // 2, 1)
    pairs = list(zip(range(cut), range(cut, chunk)))

    def turn(fine, more):
        def body(_, norms):
            norms = list(norms)
            for a, b in pairs:
                spread(b, fine)
                norms[a] = gather(a, fine, norms[a])
            for a, b in pairs:
                if more:
                    spread(a, fine)
                norms[b] = gather(b, fine, norms[b])
            return tuple(norms)

        return body

    for a, _ in pairs:
        spread(a, opening)
    turns = FINE if opening else ITERS - FINE
    norms = lax.fori_loop(0, turns - 1, turn(opening, True), tuple(norms), unroll=2)
    norms = turn(opening, False)(0, norms)
    if opening:
        for j in range(chunk):
            norm_out[j : j + 1, :] = norms[j]


def solve_call(me, keys, keyt, queries, weights, run, ridge, rest, start, chunk, place):
    opening = start is not None
    tokens = keys.shape[0]
    width = keyt.shape[1]

    def mine(a):
        zeros = (0,) * (a.ndim - 1)
        return spec((chunk, *a.shape[1:]), lambda i: (place, *zeros))

    block = spec((tokens, chunk * width), lambda i: (0, place))
    ins = [me, keys, keyt, queries, weights, run, ridge, *rest]
    in_specs = (
        [SMEM, block]
        + [mine(a) for a in ins[2:7]]
        + [whole(a.shape) for a in rest]
    )
    columns = jax.ShapeDtypeStruct((chunk, width, tokens), F)
    state = pltpu.VMEM((chunk, width, tokens), F)
    if opening:
        ins.append(start)
        in_specs.append(spec((chunk, width, width), lambda i: (place, 0, 0)))
        shapes = [
            columns,
            jax.ShapeDtypeStruct((chunk, tokens + width, 2 * width), B),
            columns,
            columns,
            jax.ShapeDtypeStruct((chunk, tokens), F),
        ]
        scratch = []
    else:
        shapes = [columns]
        scratch = [state, state]
    return pl.pallas_call(
        functools.partial(solve_kernel, chunk, width, 0, opening),
        grid=(1,),
        in_specs=in_specs,
        out_specs=[whole(s.shape) for s in shapes],
        out_shape=shapes,
        scratch_shapes=scratch
        + [
            pltpu.VMEM((chunk, 2, tokens // 2, tokens), B),
            pltpu.VMEM((chunk, 2, tokens // 2, tokens // 2), B),
            state,
        ],
        compiler_params=params(30),
        cost_estimate=cost(11 if opening else 9),
        name="solve_fine" if opening else "solve",
    )(*ins)


def readout_kernel(
    width, batch, parts, me, keys, values, weights, run, square, gain,
    mine, theirs, first, start, out_weight, count, *rest
):
    answers = rest[:parts]
    out, total = rest[parts:]
    tokens = keys.shape[0]
    i = pl.program_id(0)
    turns = pl.num_programs(0)
    c = me[0] & 1

    @pl.when(i == 0)
    def _():
        total[...] = jnp.zeros_like(total)

    at = lax.broadcasted_iota(jnp.int32, (1, tokens), 1)
    live = (at < count[0]).astype(F)
    rows = []
    for j in range(batch):
        cols = slice(j * width, (j + 1) * width)
        head = i * batch + j
        line = pl.ds(head, 1)
        answer = answers[0][j]
        for n in range(1, parts):
            answer = jnp.where(i * parts < n * turns, answer, answers[n][j])
        hi, lo = split(answer)
        both = jnp.concatenate([hi, lo], 0)
        key = keys[:, cols]
        near = (dot(jnp.concatenate([key, key], 1), both) * weights[j]).astype(B)
        value = (values[:, cols].astype(F).T * jnp.sqrt(square[line, :])).astype(B)
        memory = state_of(c, head, width, mine, theirs, first, start[j]).astype(B)
        o = jnp.exp(run[line, :]) * dot(jnp.concatenate([memory, memory], 1), both) + dot(value, near)
        scale = lax.rsqrt(jnp.mean(o * o, axis=0, keepdims=True) + 1e-05) * live
        rows.append((o * scale).T * gain[:, cols])
    y = jnp.concatenate(rows, 1).astype(B)
    total[...] += dot(y, out_weight[...])

    @pl.when(i == turns - 1)
    def _():
        out[...] = total[...].astype(B)


def readout_call(
    me, keys, values, answers, weights, run, square, gain, state, start, out_weight, count
):
    tokens = keys.shape[0]
    heads = run.shape[0]
    chunk, width, _ = answers[0].shape
    model = out_weight.shape[1]
    batch = min(chunk, BATCH)
    each = chunk // batch
    tok = spec((tokens, batch * width), lambda i: (0, i))
    ins = [me, keys, values, weights, run, square, gain.reshape(1, -1), *state, start,
           out_weight, count, *answers]

    def part(n):
        return spec(
            (batch, width, tokens), lambda i: (jnp.clip(i - n * each, 0, each - 1), 0, 0)
        )

    in_specs = [
        SMEM,
        tok,
        tok,
        stack(weights, batch),
        whole(run.shape),
        whole(square.shape),
        spec((1, batch * width), lambda i: (0, i)),
        *[whole(a.shape) for a in state],
        stack(start, batch),
        spec((batch * width, model), lambda i: (i, 0)),
        SMEM,
        *[part(n) for n in range(len(answers))],
    ]
    return pl.pallas_call(
        functools.partial(readout_kernel, width, batch, len(answers)),
        grid=(heads // batch,),
        in_specs=in_specs,
        out_specs=whole((tokens, model)),
        out_shape=jax.ShapeDtypeStruct((tokens, model), B),
        scratch_shapes=[pltpu.VMEM((tokens, model), F)],
        compiler_params=params(30),
        cost_estimate=cost(7),
        name="readout",
    )(*ins)


def local(
    shards, columns,
    queries, key_vectors, value_vectors, forget_gates, shard_counts, gram_start,
    memory_start, ridge_terms, norm_gain, out_weight,
):
    heads = forget_gates.shape[1]
    width = queries.shape[1] // heads
    chunk = min(heads, 8)
    parts = range(heads // chunk)
    me = lax.axis_index("seq").astype(jnp.int32).reshape(1)
    gates = forget_gates.T
    sums = [gram_call(shard_counts, gates, key_vectors, chunk, n) for n in parts]
    run = jnp.concatenate([a[2] for a in sums], 0)
    square = jnp.concatenate([a[3] for a in sums], 0)

    grams = [Run(prefix(me, a[0], a[1], width // 2 + 1, shards)) for a in sums]

    def advance(*late):
        for g in grams:
            if g.state is None:
                g.step(*[o.sent for o in grams if o is not g], *(late if g is grams[-1] else ()))

    advance()
    values = after(value_vectors, *[g.sent for g in grams])
    memory = Run(
        prefix(
            me,
            *memory_call(shard_counts, run, square, key_vectors, values, width, chunk),
            width,
            shards,
        )
    )
    advance()
    memory.step(grams[-1].sent)
    advance(memory.sent)
    weights, vectors, keyt, ridge = weights_call(
        shard_counts, key_vectors, after(queries, grams[0].sent), run, square, ridge_terms, width,
        chunk,
    )
    advance(vectors)
    memory.step(grams[-1].sent)
    states = [grams[0].finish(*[g.sent for g in grams[1:]], memory.sent)]

    answers = []
    last = memory.sent
    for n in parts:
        common = (weights, run, ridge)
        opened = solve_call(
            me, key_vectors, keyt, after(vectors, last, memory.sent, *[g.sent for g in grams]), *common,
            states[n], gram_start, chunk, n,
        )
        opened = list(opened)
        states += [g.finish(opened[0]) for g in grams[n + 1 : n + 2]]
        if memory.state is None:
            memory.step(opened[0])
            opened[0] = after(opened[0], memory.sent)
        answers += solve_call(me, key_vectors, keyt, vectors, *common, opened, None, chunk, n)
        last = answers[-1]
        if n == 0 and memory.state is None:
            memory.step(last)
    memory_state = memory.finish(last)
    mixed = readout_call(
        me, key_vectors, value_vectors, answers, weights, run, square, norm_gain,
        memory_state, memory_start, out_weight, shard_counts,
    )
    if columns > 1:
        mixed = lax.psum_scatter(mixed, "head", scatter_dimension=1, tiled=True)
    return mixed


def solution(mesh):
    return jax.shard_map(
        functools.partial(local, mesh.shape["seq"], mesh.shape["head"]),
        mesh=mesh,
        in_specs=(
            P("seq", "head"),
            P("seq", "head"),
            P("seq", "head"),
            P("seq", "head"),
            P("seq"),
            P("head", None, None),
            P("head", None, None),
            P("head", None),
            P("head"),
            P("head", None),
        ),
        out_specs=P("seq", "head"),
        check_vma=False,
    )
```

```python
import functools

import jax
import jax.numpy as jnp
from jax import lax
from jax.experimental import pallas as pl
from jax.experimental.pallas import tpu as pltpu
from jax.sharding import PartitionSpec as P

ITERS = 16
FINE = 9
BATCH = 8
EARLY = 2
F = jnp.float32
B = jnp.bfloat16
DEAD = 1e30
MIB = 1 << 20


def split(a):
    hi = a.astype(B)
    return hi, (a - hi.astype(F)).astype(B)


def dot(a, b):
    return jnp.dot(a, b, preferred_element_type=F)


def spec(block, index):
    return pl.BlockSpec(block, index)


def whole(shape):
    zeros = (0,) * len(shape)
    return pl.BlockSpec(shape, lambda *_: zeros)


SMEM = pl.BlockSpec(memory_space=pltpu.SMEM)


def params(mib):
    return pltpu.CompilerParams(vmem_limit_bytes=mib * MIB)


def cost(us):
    return pl.CostEstimate(flops=int(us * 1e9), bytes_accessed=int(us * 1e6), transcendentals=0)


def split_rows(tail, decay, lead):
    first = decay.astype(B).astype(F)
    second = (decay - first).astype(B).astype(F)
    third = decay - first - second
    row = lax.broadcasted_iota(jnp.int32, tail, 0)
    n = 0
    out = jnp.zeros(tail, F)
    if lead is not None:
        out = jnp.where(row == 0, lead, out)
        n = 1
    for value in (first, second, third):
        out = jnp.where(row == n, value, out)
        n += 1
    return out.astype(B)


def emit(sums_out, pay_out, j, body, decay, lead):
    height = body.shape[0]
    width = body.shape[1]
    sums_out[j, :height] = body
    row = lax.broadcasted_iota(jnp.int32, (16, width), 0)
    wide = jnp.broadcast_to(decay, (16, width))
    sums_out[j, height:] = wide if lead is None else jnp.where(row == 0, lead, wide)
    if pay_out is not None:
        pay_out[j, :height] = body.astype(B)
        pay_out[j, height:] = split_rows((16, width), wide, lead)


def pack(gram):
    half = gram.shape[0] // 2
    turned = pltpu.roll(gram[half:], half, 1)
    row = lax.broadcasted_iota(jnp.int32, turned.shape, 0)
    col = lax.broadcasted_iota(jnp.int32, turned.shape, 1)
    body = jnp.where((col < half) & (row < col), turned, gram[:half])
    diagonal = jnp.sum(jnp.where(row == col, turned, 0.0), axis=0, keepdims=True)
    return body, diagonal


def unpack(body, diagonal):
    half, width = body.shape
    flipped = jnp.concatenate([body, jnp.zeros_like(body)], 0).T
    row = lax.broadcasted_iota(jnp.int32, body.shape, 0)
    col = lax.broadcasted_iota(jnp.int32, body.shape, 1)
    top = jnp.where((col < half) & (row < col), flipped[:half], body)
    corner = jnp.where(row < col, body, jnp.where(row == col, diagonal, flipped[:half]))
    low = jnp.where(col < half, flipped[half:], pltpu.roll(corner, half, 1))
    return jnp.concatenate([top, low], 0)


def gram_kernel(chunk, width, count, gates, keys, sums_out, pay_out, run_out, square_out):
    tokens = keys.shape[0]
    at = lax.broadcasted_iota(jnp.int32, (1, tokens), 1)
    live = at < count[0]
    row = lax.broadcasted_iota(jnp.int32, (tokens, tokens), 0)
    col = lax.broadcasted_iota(jnp.int32, (tokens, tokens), 1)
    run = jnp.dot(
        jnp.where(live, jnp.log(gates[...]), 0.0),
        (row <= col).astype(F),
        preferred_element_type=F,
        precision=lax.Precision.HIGHEST,
    )
    run_out[...] = run
    for j in range(chunk):
        key = keys[:, j * width : (j + 1) * width]
        keyt = key.astype(F).T
        square = jnp.sum(keyt * keyt, axis=0, keepdims=True) + 1e-06
        now = run[j : j + 1]
        last = now[:, tokens - 1 :]
        tail = jnp.where(live, jnp.exp(last - now), 0.0)
        square_out[j : j + 1, :] = square
        hi, lo = split(keyt * (tail / square))
        gram = dot(jnp.concatenate([hi, lo], 1), jnp.concatenate([key, key], 0))
        body, diagonal = pack(gram)
        emit(sums_out, pay_out, j, body, jnp.broadcast_to(jnp.exp(last), (1, width)), diagonal)


def stack(a, chunk):
    block = (chunk, *a.shape[1:])
    zeros = (0,) * (len(block) - 1)
    return pl.BlockSpec(block, lambda i: (i, *zeros))


def gram_call(count, gates, keys, chunk, place):
    tokens = keys.shape[0]
    heads = gates.shape[0]
    width = keys.shape[1] // heads
    rows = width // 2 + 16
    shapes = [
        jax.ShapeDtypeStruct((chunk, rows, width), F),
        jax.ShapeDtypeStruct((chunk, rows, width), B),
        jax.ShapeDtypeStruct((chunk, tokens), F),
        jax.ShapeDtypeStruct((chunk, tokens), F),
    ]
    return pl.pallas_call(
        functools.partial(gram_kernel, chunk, width),
        grid=(1,),
        in_specs=[
            SMEM,
            spec((chunk, tokens), lambda i: (place, 0)),
            spec((tokens, chunk * width), lambda i: (0, place)),
        ],
        out_specs=[stack(s, chunk) for s in shapes],
        out_shape=shapes,
        compiler_params=params(16),
        cost_estimate=cost(3),
        name="gram_sums",
    )(count, gates, keys)


def memory_kernel(chunk, width, count, run, square, keys, values, sums_out, pay_out):
    tokens = keys.shape[0]
    at = lax.broadcasted_iota(jnp.int32, (1, tokens), 1)
    live = at < count[0]
    for j in range(chunk):
        cols = slice(j * width, (j + 1) * width)
        key = keys[:, cols]
        now = run[j : j + 1]
        last = now[:, tokens - 1 :]
        tail = jnp.where(live, jnp.exp(last - now), 0.0)
        hi, lo = split(values[:, cols].astype(F).T * (tail * lax.rsqrt(square[j : j + 1])))
        memory = dot(jnp.concatenate([hi, lo], 1), jnp.concatenate([key, key], 0))
        emit(sums_out, pay_out, j, memory, jnp.broadcast_to(jnp.exp(last), (1, width)), None)


def memory_call(count, run, square, keys, values, width, chunk):
    tokens = keys.shape[0]
    heads = run.shape[0]
    block = spec((tokens, chunk * width), lambda i: (0, i))
    shapes = [
        jax.ShapeDtypeStruct((heads, width + 16, width), F),
        jax.ShapeDtypeStruct((heads, width + 16, width), B),
    ]
    return pl.pallas_call(
        functools.partial(memory_kernel, chunk, width),
        grid=(heads // chunk,),
        in_specs=[SMEM, stack(run, chunk), stack(square, chunk), block, block],
        out_specs=[stack(s, chunk) for s in shapes],
        out_shape=shapes,
        compiler_params=params(16),
        cost_estimate=cost(2),
        name="memory_sums",
    )(count, run, square, keys, values)


def decay_of(tail, off):
    return tail[off : off + 1] + tail[off + 1 : off + 2] + tail[off + 2 : off + 3]


def fold_kernel(half, data, bit, final, me, total, got, *rest):
    width = total.shape[2]
    body = data // 16 * 16
    off = data - body
    side = me[0] & 1
    up = ((me[0] >> bit) & 1) == 1
    rest = list(rest)
    before = rest.pop(0) if bit > 1 else None
    for j in range(half):
        at = side * half + j if bit == 0 else j
        tail = got[at, body:].astype(F)
        theirs = decay_of(tail, off)
        mine = total[at, data : data + 1]
        other = got[at, :body].astype(F)
        if not final:
            keep = jnp.where(up, 1.0, theirs)
            take = jnp.where(up, mine, 1.0)
            lead = keep * total[at, body : body + 1] + take * tail[:1] if off else None
            emit(
                rest[0], rest[1], j, keep * total[at, :body] + take * other, mine * theirs, lead
            )
        if bit > 0:
            gate = jnp.where(up, 1.0, 0.0)
            if before is None:
                inner, lead, decay = gate * other, gate * tail[:1], jnp.where(up, theirs, 1.0)
            else:
                scale = gate * before[j, data : data + 1]
                inner = scale * other + before[j, :body]
                lead = scale * tail[:1] + before[j, body : body + 1]
                decay = before[j, data : data + 1] * jnp.where(up, theirs, 1.0)
            emit(rest[-1], None, j, inner, decay, lead if off else None)


def fold(me, total, got, before, data, bit, final):
    half = got.shape[0] // 2 if bit == 0 else got.shape[0]
    _, rows, width = total.shape
    sums = jax.ShapeDtypeStruct((half, rows, width), F)
    ins = [me, total, got] + ([] if before is None else [before])
    shapes = ([] if final else [sums, jax.ShapeDtypeStruct((half, rows, width), B)]) + (
        [] if bit == 0 else [sums]
    )
    return pl.pallas_call(
        functools.partial(fold_kernel, half, data, bit, final),
        in_specs=[SMEM] + [whole(a.shape) for a in ins[1:]],
        out_specs=[whole(s.shape) for s in shapes],
        out_shape=shapes,
        compiler_params=params(16),
        cost_estimate=cost(1),
        name="fold",
    )(*ins)


def after(a, *others):
    return lax.optimization_barrier((a, *others))[0]


def prefix(me, sums, pay, data, shards):
    first = lax.ppermute(pay, "seq", [(i, i ^ 1) for i in range(shards)])
    late = yield pay
    first = after(first, *late)
    total, got, before = sums, first, None
    bit = 0
    while True:
        final = 2 << bit >= shards
        outs = fold(me, total, got, before, data, bit, final)
        if bit > 0:
            before = outs[-1]
        if final:
            break
        total, pay = outs[:2]
        bit += 1
        stride = 1 << bit
        moves = [(i, i ^ stride) for i in range(shards)]
        if stride * 2 >= shards:
            moves = [m for m in moves if m[0] < m[1]]
        got = lax.ppermute(pay, "seq", moves)
        late = yield pay
        got = after(got, *late)
    theirs = lax.ppermute(before, "seq", [(i, i ^ 1) for i in range(shards)])
    late = yield before
    theirs = after(theirs, *late)
    yield before, theirs, first


class Run:
    def __init__(self, steps):
        self.steps = steps
        self.sent = next(steps)
        self.state = None

    def step(self, *late):
        out = self.steps.send(late)
        if isinstance(out, tuple):
            self.state = out
        else:
            self.sent = out
        return self

    def finish(self, *late):
        while self.state is None:
            self.step(*late)
            late = ()
        return self.state


def state_of(c, head, data, mine, theirs, first, start):
    half = mine.shape[0]
    at = lax.rem(jnp.int32(head), jnp.int32(half))
    same = c == lax.div(jnp.int32(head), jnp.int32(half))
    body = data // 16 * 16
    off = data - body
    before = jnp.where(same, mine[at], theirs[at])
    tail = first[head, body:].astype(F)
    decay = jnp.where(c == 0, 1.0, decay_of(tail, off))
    scale = jnp.where(c == 0, 0.0, 1.0)
    rows = decay * before[:body] + scale * first[head, :body].astype(F)
    if off:
        diagonal = decay * before[body : body + 1] + scale * tail[:1]
        rows = unpack(rows, diagonal)
    return rows + (decay * before[data : data + 1]) * start


def weights_kernel(
    chunk, width, count, keys, queries, run, square, ridge, weight_out, query_out, keyt_out,
    ridge_out, wide,
):
    tokens = queries.shape[0]
    at = lax.broadcasted_iota(jnp.int32, (1, tokens), 1)
    now = run[...]
    wide[...] = jnp.zeros_like(wide)
    wide[:chunk] = jnp.where(at < count[0], now + jnp.log(square[...]), DEAD)
    tall = wide[...].T
    row = lax.broadcasted_iota(jnp.int32, (tokens, tokens), 0)
    col = lax.broadcasted_iota(jnp.int32, (tokens, tokens), 1)
    for j in range(chunk):
        weight_out[j] = jnp.where(row <= col, jnp.exp(now[j : j + 1] - tall[:, j : j + 1]), 0.0)
        cols = slice(j * width, (j + 1) * width)
        keyt_out[j] = keys[:, cols].T
        ridge_out[j] = jnp.broadcast_to(ridge[j : j + 1], (width, width)).T
        q = queries[:, cols].astype(F).T
        query_out[j] = q * lax.rsqrt(jnp.sum(q * q, axis=0, keepdims=True) + 1e-06)


def weights_call(count, keys, queries, run, square, ridge, width, chunk):
    tokens = queries.shape[0]
    heads = run.shape[0]
    shapes = [
        jax.ShapeDtypeStruct((heads, tokens, tokens), F),
        jax.ShapeDtypeStruct((heads, width, tokens), F),
        jax.ShapeDtypeStruct((heads, width, tokens), B),
        jax.ShapeDtypeStruct((heads, width, width), F),
    ]
    block = spec((tokens, chunk * width), lambda i: (0, i))
    return pl.pallas_call(
        functools.partial(weights_kernel, chunk, width),
        grid=(heads // chunk,),
        in_specs=[
            SMEM,
            block,
            block,
            stack(run, chunk),
            stack(square, chunk),
            stack(ridge, chunk),
        ],
        out_specs=[stack(s, chunk) for s in shapes],
        out_shape=shapes,
        scratch_shapes=[pltpu.VMEM((128, tokens), F)],
        compiler_params=params(20),
        cost_estimate=cost(2),
        name="weights",
    )(count, keys, queries, run, square, ridge)


def solve_kernel(
    chunk, width, base, opening, coarse, me, keys, keyt, queries, weights, run, ridge, *rest
):
    tokens = keys.shape[0]
    half_t = tokens // 2
    c = me[0] & 1
    if opening:
        mine, theirs, first, start, answer_out, left, dirs, resid, norm_out, *rest = rest
    else:
        answer_in, left, dirs_in, resid_in, norm_in, answer_out, dirs, resid, *rest = rest
    near_top, near_low, far = rest
    lead = []
    norms = []
    for j in range(chunk):
        lead.append(jnp.exp(run[j : j + 1, :]))
        if not opening:
            dirs[j] = dirs_in[j]
            resid[j] = resid_in[j]
            answer_out[j] = answer_in[j]
            norms.append(norm_in[j : j + 1, :])
            continue
        key = keys[:, j * width : (j + 1) * width]
        left[j, :tokens, :width] = key
        left[j, :tokens, width:] = key
        gram = state_of(c, base + j, width // 2 + 1, mine, theirs, first, start[j]).astype(B)
        left[j, tokens:, :width] = gram
        left[j, tokens:, width:] = gram
        q = queries[j]
        dirs[j] = q
        resid[j] = q
        answer_out[j] = jnp.zeros_like(q)
        norms.append(jnp.sum(q * q, axis=0, keepdims=True))

    def spread(j, fine):
        p = dirs[j]
        if fine:
            hi, lo = split(p)
            image = dot(left[j], jnp.concatenate([hi, lo], 0))
        else:
            image = dot(left[j, :, :width], p.astype(B))
        far[j] = image[tokens:]
        top = image[:half_t] * weights[j, :half_t]
        low = image[half_t:tokens, half_t:] * weights[j, half_t:, half_t:]
        if fine:
            near_top[j, 0], near_top[j, 1] = split(top)
            near_low[j, 0], near_low[j, 1] = split(low)
        else:
            near_top[j, 0] = top.astype(B)
            near_low[j, 0] = low.astype(B)

    def gather(j, fine, norm):
        kt = keyt[j]
        p = dirs[j]
        if fine:
            early = kt[:, :half_t]
            one = dot(
                jnp.concatenate([early, early], 1),
                jnp.concatenate([near_top[j, 0, :, :half_t], near_top[j, 1, :, :half_t]], 0),
            )
            two = dot(
                kt,
                jnp.concatenate(
                    [
                        jnp.concatenate([near_top[j, 0, :, half_t:], near_top[j, 1, :, half_t:]], 1),
                        jnp.concatenate([near_low[j, 0], near_low[j, 1]], 1),
                    ],
                    0,
                ),
            )
            near = jnp.concatenate([one, two[:, :half_t] + two[:, half_t:]], 1)
        else:
            low = near_low[j, 0]
            near = dot(
                kt,
                jnp.concatenate(
                    [near_top[j, 0], jnp.concatenate([jnp.zeros_like(low), low], 1)], 0
                ),
            )
        image = lead[j] * far[j] + near + jnp.concatenate([ridge[j]] * (tokens // width), 1) * p
        step = norm / jnp.sum(p * image, axis=0, keepdims=True)
        answer_out[j] = answer_out[j] + step * p
        r = resid[j] - step * image
        resid[j] = r
        after = jnp.sum(r * r, axis=0, keepdims=True)
        dirs[j] = r + (after / norm) * p
        return after

    cut = max(chunk // 2, 1)
    pairs = list(zip(range(cut), range(cut, chunk)))

    def turn(fine, then):
        def body(_, norms):
            norms = list(norms)
            for a, b in pairs:
                spread(b, fine)
                norms[a] = gather(a, fine, norms[a])
            for a, b in pairs:
                if then is not None:
                    spread(a, then)
                norms[b] = gather(b, fine, norms[b])
            return tuple(norms)

        return body

    kinds = ([(True, FINE)] if opening else []) + ([(False, coarse)] if coarse else [])
    for a, _ in pairs:
        spread(a, kinds[0][0])
    norms = tuple(norms)
    for n, (kind, turns) in enumerate(kinds):
        norms = lax.fori_loop(0, turns - 1, turn(kind, kind), norms, unroll=4)
        norms = turn(kind, kinds[n + 1][0] if n + 1 < len(kinds) else None)(0, norms)
    if opening:
        for j in range(chunk):
            norm_out[j : j + 1, :] = norms[j]


def solve_call(
    me, keys, keyt, queries, weights, run, ridge, rest, start, coarse, chunk, place
):
    opening = start is not None
    tokens = keys.shape[0]
    width = keyt.shape[1]

    def mine(a):
        zeros = (0,) * (a.ndim - 1)
        return spec((chunk, *a.shape[1:]), lambda i: (place, *zeros))

    block = spec((tokens, chunk * width), lambda i: (0, place))
    ins = [me, keys, keyt, queries, weights, run, ridge, *rest]
    in_specs = (
        [SMEM, block]
        + [mine(a) for a in ins[2:7]]
        + [whole(a.shape) for a in rest]
    )
    columns = jax.ShapeDtypeStruct((chunk, width, tokens), F)
    state = pltpu.VMEM((chunk, width, tokens), F)
    if opening:
        ins.append(start)
        in_specs.append(spec((chunk, width, width), lambda i: (place, 0, 0)))
        shapes = [
            columns,
            jax.ShapeDtypeStruct((chunk, tokens + width, 2 * width), B),
            columns,
            columns,
            jax.ShapeDtypeStruct((chunk, tokens), F),
        ]
        scratch = []
    else:
        shapes = [columns]
        scratch = [state, state]
    return pl.pallas_call(
        functools.partial(solve_kernel, chunk, width, 0, opening, coarse),
        grid=(1,),
        in_specs=in_specs,
        out_specs=[whole(s.shape) for s in shapes],
        out_shape=shapes,
        scratch_shapes=scratch
        + [
            pltpu.VMEM((chunk, 2, tokens // 2, tokens), B),
            pltpu.VMEM((chunk, 2, tokens // 2, tokens // 2), B),
            state,
        ],
        compiler_params=params(30),
        cost_estimate=cost(11 if opening else 9),
        name="solve_fine" if opening else "solve",
    )(*ins)


def readout_kernel(
    width, batch, parts, me, keys, values, weights, run, square, gain,
    mine, theirs, first, start, out_weight, count, *rest
):
    answers = rest[:parts]
    out, total = rest[parts:]
    tokens = keys.shape[0]
    i = pl.program_id(0)
    turns = pl.num_programs(0)
    c = me[0] & 1

    @pl.when(i == 0)
    def _():
        total[...] = jnp.zeros_like(total)

    at = lax.broadcasted_iota(jnp.int32, (1, tokens), 1)
    live = (at < count[0]).astype(F)
    rows = []
    for j in range(batch):
        cols = slice(j * width, (j + 1) * width)
        head = i * batch + j
        line = pl.ds(head, 1)
        answer = answers[0][j]
        for n in range(1, parts):
            answer = jnp.where(i * parts < n * turns, answer, answers[n][j])
        hi, lo = split(answer)
        both = jnp.concatenate([hi, lo], 0)
        key = keys[:, cols]
        near = (dot(jnp.concatenate([key, key], 1), both) * weights[j]).astype(B)
        value = (values[:, cols].astype(F).T * jnp.sqrt(square[line, :])).astype(B)
        memory = state_of(c, head, width, mine, theirs, first, start[j]).astype(B)
        o = jnp.exp(run[line, :]) * dot(jnp.concatenate([memory, memory], 1), both) + dot(value, near)
        scale = lax.rsqrt(jnp.mean(o * o, axis=0, keepdims=True) + 1e-05) * live
        rows.append((o * scale).T * gain[:, cols])
    y = jnp.concatenate(rows, 1).astype(B)
    total[...] += dot(y, out_weight[...])

    @pl.when(i == turns - 1)
    def _():
        out[...] = total[...].astype(B)


def readout_call(
    me, keys, values, answers, weights, run, square, gain, state, start, out_weight, count
):
    tokens = keys.shape[0]
    heads = run.shape[0]
    chunk, width, _ = answers[0].shape
    model = out_weight.shape[1]
    batch = min(chunk, BATCH)
    each = chunk // batch
    tok = spec((tokens, batch * width), lambda i: (0, i))
    ins = [me, keys, values, weights, run, square, gain.reshape(1, -1), *state, start,
           out_weight, count, *answers]

    def part(n):
        return spec(
            (batch, width, tokens), lambda i: (jnp.clip(i - n * each, 0, each - 1), 0, 0)
        )

    in_specs = [
        SMEM,
        tok,
        tok,
        stack(weights, batch),
        whole(run.shape),
        whole(square.shape),
        spec((1, batch * width), lambda i: (0, i)),
        *[whole(a.shape) for a in state],
        stack(start, batch),
        spec((batch * width, model), lambda i: (i, 0)),
        SMEM,
        *[part(n) for n in range(len(answers))],
    ]
    return pl.pallas_call(
        functools.partial(readout_kernel, width, batch, len(answers)),
        grid=(heads // batch,),
        in_specs=in_specs,
        out_specs=whole((tokens, model)),
        out_shape=jax.ShapeDtypeStruct((tokens, model), B),
        scratch_shapes=[pltpu.VMEM((tokens, model), F)],
        compiler_params=params(30),
        cost_estimate=cost(7),
        name="readout",
    )(*ins)


def local(
    shards, columns,
    queries, key_vectors, value_vectors, forget_gates, shard_counts, gram_start,
    memory_start, ridge_terms, norm_gain, out_weight,
):
    heads = forget_gates.shape[1]
    width = queries.shape[1] // heads
    chunk = min(heads, 8)
    parts = range(heads // chunk)
    me = lax.axis_index("seq").astype(jnp.int32).reshape(1)
    gates = forget_gates.T
    sums = [gram_call(shard_counts, gates, key_vectors, chunk, n) for n in parts]
    run = jnp.concatenate([a[2] for a in sums], 0)
    square = jnp.concatenate([a[3] for a in sums], 0)

    grams = [Run(prefix(me, a[0], a[1], width // 2 + 1, shards)) for a in sums]

    def advance(*late):
        for g in grams:
            if g.state is None:
                g.step(*[o.sent for o in grams if o is not g], *(late if g is grams[-1] else ()))

    advance()
    values = after(value_vectors, *[g.sent for g in grams])
    memory = Run(
        prefix(
            me,
            *memory_call(shard_counts, run, square, key_vectors, values, width, chunk),
            width,
            shards,
        )
    )
    advance()
    memory.step(grams[-1].sent)
    advance(memory.sent)
    weights, vectors, keyt, ridge = weights_call(
        shard_counts, key_vectors, after(queries, grams[0].sent), run, square, ridge_terms, width,
        chunk,
    )
    advance(vectors)
    memory.step(grams[-1].sent)
    states = [grams[0].finish(*[g.sent for g in grams[1:]], memory.sent)]

    answers = []
    last = memory.sent
    for n in parts:
        common = (weights, run, ridge)
        early = EARLY if n == len(parts) - 1 else 0
        opened = solve_call(
            me, key_vectors, keyt, after(vectors, last, memory.sent, *[g.sent for g in grams]), *common,
            states[n], gram_start, early, chunk, n,
        )
        opened = list(opened)
        states += [g.finish(opened[0]) for g in grams[n + 1 : n + 2]]
        if memory.state is None:
            memory.step(opened[0])
            opened[0] = after(opened[0], memory.sent)
        answers += solve_call(
            me, key_vectors, keyt, vectors, *common, opened, None, ITERS - FINE - early, chunk, n
        )
        last = answers[-1]
        if n == 0 and memory.state is None:
            memory.step(last)
    memory_state = memory.finish(last)
    mixed = readout_call(
        me, key_vectors, value_vectors, answers, weights, run, square, norm_gain,
        memory_state, memory_start, out_weight, shard_counts,
    )
    if columns > 1:
        mixed = lax.psum_scatter(mixed, "head", scatter_dimension=1, tiled=True)
    return mixed


def solution(mesh):
    return jax.shard_map(
        functools.partial(local, mesh.shape["seq"], mesh.shape["head"]),
        mesh=mesh,
        in_specs=(
            P("seq", "head"),
            P("seq", "head"),
            P("seq", "head"),
            P("seq", "head"),
            P("seq"),
            P("head", None, None),
            P("head", None, None),
            P("head", None),
            P("head"),
            P("head", None),
        ),
        out_specs=P("seq", "head"),
        check_vma=False,
    )
```

```python
import functools

import jax
import jax.numpy as jnp
from jax import lax
from jax.experimental import pallas as pl
from jax.experimental.pallas import tpu as pltpu
from jax.sharding import PartitionSpec as P


ITERS = 16
FINE = 9
BATCH = 8
EARLY = 2
F = jnp.float32
B = jnp.bfloat16
DEAD = 1e30
MIB = 1 << 20


def split(a):
    hi = a.astype(B)
    return hi, (a - hi.astype(F)).astype(B)


def dot(a, b):
    return jnp.dot(a, b, preferred_element_type=F)


def spec(block, index):
    return pl.BlockSpec(block, index)


def whole(shape):
    zeros = (0,) * len(shape)
    return pl.BlockSpec(shape, lambda *_: zeros)


SMEM = pl.BlockSpec(memory_space=pltpu.SMEM)


def params(mib):
    return pltpu.CompilerParams(vmem_limit_bytes=mib * MIB)


def cost(us):
    return pl.CostEstimate(flops=int(us * 1e9), bytes_accessed=int(us * 1e6), transcendentals=0)


def split_rows(tail, decay, lead):
    first = decay.astype(B).astype(F)
    second = (decay - first).astype(B).astype(F)
    third = decay - first - second
    row = lax.broadcasted_iota(jnp.int32, tail, 0)
    n = 0
    out = jnp.zeros(tail, F)
    if lead is not None:
        out = jnp.where(row == 0, lead, out)
        n = 1
    for value in (first, second, third):
        out = jnp.where(row == n, value, out)
        n += 1
    return out.astype(B)


def emit(sums_out, pay_out, j, body, decay, lead):
    height = body.shape[0]
    width = body.shape[1]
    sums_out[j, :height] = body
    row = lax.broadcasted_iota(jnp.int32, (16, width), 0)
    wide = jnp.broadcast_to(decay, (16, width))
    sums_out[j, height:] = wide if lead is None else jnp.where(row == 0, lead, wide)
    if pay_out is not None:
        pay_out[j, :height] = body.astype(B)
        pay_out[j, height:] = split_rows((16, width), wide, lead)


def pack(gram):
    half = gram.shape[0] // 2
    turned = pltpu.roll(gram[half:], half, 1)
    row = lax.broadcasted_iota(jnp.int32, turned.shape, 0)
    col = lax.broadcasted_iota(jnp.int32, turned.shape, 1)
    body = jnp.where((col < half) & (row < col), turned, gram[:half])
    diagonal = jnp.sum(jnp.where(row == col, turned, 0.0), axis=0, keepdims=True)
    return body, diagonal


def unpack(body, diagonal):
    half, _ = body.shape
    flipped = jnp.concatenate([body, jnp.zeros_like(body)], 0).T
    row = lax.broadcasted_iota(jnp.int32, body.shape, 0)
    col = lax.broadcasted_iota(jnp.int32, body.shape, 1)
    top = jnp.where((col < half) & (row < col), flipped[:half], body)
    corner = jnp.where(row < col, body, jnp.where(row == col, diagonal, flipped[:half]))
    low = jnp.where(col < half, flipped[half:], pltpu.roll(corner, half, 1))
    return jnp.concatenate([top, low], 0)


def gram_kernel(chunk, width, count, gates, keys, sums_out, pay_out, run_out, square_out):
    tokens = keys.shape[0]
    at = lax.broadcasted_iota(jnp.int32, (1, tokens), 1)
    live = at < count[0]
    row = lax.broadcasted_iota(jnp.int32, (tokens, tokens), 0)
    col = lax.broadcasted_iota(jnp.int32, (tokens, tokens), 1)
    run = jnp.dot(
        jnp.where(live, jnp.log(gates[...]), 0.0),
        (row <= col).astype(F),
        preferred_element_type=F,
        precision=lax.Precision.HIGHEST,
    )
    run_out[...] = run
    for j in range(chunk):
        key = keys[:, j * width : (j + 1) * width]
        keyt = key.astype(F).T
        square = jnp.sum(keyt * keyt, axis=0, keepdims=True) + 1e-06
        now = run[j : j + 1]
        last = now[:, tokens - 1 :]
        tail = jnp.where(live, jnp.exp(last - now), 0.0)
        square_out[j : j + 1, :] = square
        hi, lo = split(keyt * (tail / square))
        gram = dot(jnp.concatenate([hi, lo], 1), jnp.concatenate([key, key], 0))
        body, diagonal = pack(gram)
        emit(sums_out, pay_out, j, body, jnp.broadcast_to(jnp.exp(last), (1, width)), diagonal)


def stack(a, chunk):
    block = (chunk, *a.shape[1:])
    zeros = (0,) * (len(block) - 1)
    return pl.BlockSpec(block, lambda i: (i, *zeros))


def gram_call(count, gates, keys, chunk, place):
    tokens = keys.shape[0]
    heads = gates.shape[0]
    width = keys.shape[1] // heads
    rows = width // 2 + 16
    shapes = [
        jax.ShapeDtypeStruct((chunk, rows, width), F),
        jax.ShapeDtypeStruct((chunk, rows, width), B),
        jax.ShapeDtypeStruct((chunk, tokens), F),
        jax.ShapeDtypeStruct((chunk, tokens), F),
    ]
    return pl.pallas_call(
        functools.partial(gram_kernel, chunk, width),
        grid=(1,),
        in_specs=[
            SMEM,
            spec((chunk, tokens), lambda i: (place, 0)),
            spec((tokens, chunk * width), lambda i: (0, place)),
        ],
        out_specs=[stack(s, chunk) for s in shapes],
        out_shape=shapes,
        compiler_params=params(16),
        cost_estimate=cost(3),
        name="gram_sums",
    )(count, gates, keys)


def memory_kernel(chunk, width, count, run, square, keys, values, sums_out, pay_out):
    tokens = keys.shape[0]
    at = lax.broadcasted_iota(jnp.int32, (1, tokens), 1)
    live = at < count[0]
    for j in range(chunk):
        cols = slice(j * width, (j + 1) * width)
        key = keys[:, cols]
        now = run[j : j + 1]
        last = now[:, tokens - 1 :]
        tail = jnp.where(live, jnp.exp(last - now), 0.0)
        hi, lo = split(values[:, cols].astype(F).T * (tail * lax.rsqrt(square[j : j + 1])))
        memory = dot(jnp.concatenate([hi, lo], 1), jnp.concatenate([key, key], 0))
        emit(sums_out, pay_out, j, memory, jnp.broadcast_to(jnp.exp(last), (1, width)), None)


def memory_call(count, run, square, keys, values, width, chunk):
    tokens = keys.shape[0]
    heads = run.shape[0]
    block = spec((tokens, chunk * width), lambda i: (0, i))
    shapes = [
        jax.ShapeDtypeStruct((heads, width + 16, width), F),
        jax.ShapeDtypeStruct((heads, width + 16, width), B),
    ]
    return pl.pallas_call(
        functools.partial(memory_kernel, chunk, width),
        grid=(heads // chunk,),
        in_specs=[SMEM, stack(run, chunk), stack(square, chunk), block, block],
        out_specs=[stack(s, chunk) for s in shapes],
        out_shape=shapes,
        compiler_params=params(16),
        cost_estimate=cost(2),
        name="memory_sums",
    )(count, run, square, keys, values)


def decay_of(tail, off):
    return tail[off : off + 1] + tail[off + 1 : off + 2] + tail[off + 2 : off + 3]


def fold_kernel(half, data, bit, final, me, total, got, *rest):
    body = data // 16 * 16
    off = data - body
    side = me[0] & 1
    up = ((me[0] >> bit) & 1) == 1
    rest = list(rest)
    before = rest.pop(0) if bit > 1 else None
    for j in range(half):
        at = side * half + j if bit == 0 else j
        tail = got[at, body:].astype(F)
        theirs = decay_of(tail, off)
        mine = total[at, data : data + 1]
        other = got[at, :body].astype(F)
        if not final:
            keep = jnp.where(up, 1.0, theirs)
            take = jnp.where(up, mine, 1.0)
            lead = keep * total[at, body : body + 1] + take * tail[:1] if off else None
            emit(
                rest[0], rest[1], j, keep * total[at, :body] + take * other, mine * theirs, lead
            )
        if bit > 0:
            gate = jnp.where(up, 1.0, 0.0)
            if before is None:
                inner, lead, decay = gate * other, gate * tail[:1], jnp.where(up, theirs, 1.0)
            else:
                scale = gate * before[j, data : data + 1]
                inner = scale * other + before[j, :body]
                lead = scale * tail[:1] + before[j, body : body + 1]
                decay = before[j, data : data + 1] * jnp.where(up, theirs, 1.0)
            emit(rest[-1], None, j, inner, decay, lead if off else None)


def fold(me, total, got, before, data, bit, final):
    half = got.shape[0] // 2 if bit == 0 else got.shape[0]
    _, rows, width = total.shape
    sums = jax.ShapeDtypeStruct((half, rows, width), F)
    ins = [me, total, got] + ([] if before is None else [before])
    shapes = ([] if final else [sums, jax.ShapeDtypeStruct((half, rows, width), B)]) + (
        [] if bit == 0 else [sums]
    )
    return pl.pallas_call(
        functools.partial(fold_kernel, half, data, bit, final),
        in_specs=[SMEM] + [whole(a.shape) for a in ins[1:]],
        out_specs=[whole(s.shape) for s in shapes],
        out_shape=shapes,
        compiler_params=params(16),
        cost_estimate=cost(1),
        name="fold",
    )(*ins)


def after(a, *others):
    return lax.optimization_barrier((a, *others))[0]


def prefix(me, sums, pay, data, shards):
    first = lax.ppermute(pay, "seq", [(i, i ^ 1) for i in range(shards)])
    late = yield pay
    first = after(first, *late)
    total, got, before = sums, first, None
    bit = 0
    while True:
        final = 2 << bit >= shards
        outs = fold(me, total, got, before, data, bit, final)
        if bit > 0:
            before = outs[-1]
        if final:
            break
        total, pay = outs[:2]
        bit += 1
        stride = 1 << bit
        moves = [(i, i ^ stride) for i in range(shards)]
        if stride * 2 >= shards:
            moves = [m for m in moves if m[0] < m[1]]
        got = lax.ppermute(pay, "seq", moves)
        late = yield pay
        got = after(got, *late)
    theirs = lax.ppermute(before, "seq", [(i, i ^ 1) for i in range(shards)])
    late = yield before
    theirs = after(theirs, *late)
    yield before, theirs, first


class Run:
    def __init__(self, steps):
        self.steps = steps
        self.sent = next(steps)
        self.state = None

    def step(self, *late):
        out = self.steps.send(late)
        if isinstance(out, tuple):
            self.state = out
        else:
            self.sent = out
        return self

    def finish(self, *late):
        while self.state is None:
            self.step(*late)
            late = ()
        return self.state


def state_of(c, head, data, mine, theirs, first, start):
    half = mine.shape[0]
    at = lax.rem(jnp.int32(head), jnp.int32(half))
    same = c == lax.div(jnp.int32(head), jnp.int32(half))
    body = data // 16 * 16
    off = data - body
    before = jnp.where(same, mine[at], theirs[at])
    tail = first[head, body:].astype(F)
    decay = jnp.where(c == 0, 1.0, decay_of(tail, off))
    scale = jnp.where(c == 0, 0.0, 1.0)
    rows = decay * before[:body] + scale * first[head, :body].astype(F)
    if off:
        diagonal = decay * before[body : body + 1] + scale * tail[:1]
        rows = unpack(rows, diagonal)
    return rows + (decay * before[data : data + 1]) * start


def weights_kernel(
    chunk, width, count, keys, queries, run, square, ridge, weight_out, query_out, keyt_out,
    ridge_out, wide,
):
    tokens = queries.shape[0]
    at = lax.broadcasted_iota(jnp.int32, (1, tokens), 1)
    now = run[...]
    wide[...] = jnp.zeros_like(wide)
    wide[:chunk] = jnp.where(at < count[0], now + jnp.log(square[...]), DEAD)
    tall = wide[...].T
    row = lax.broadcasted_iota(jnp.int32, (tokens, tokens), 0)
    col = lax.broadcasted_iota(jnp.int32, (tokens, tokens), 1)
    for j in range(chunk):
        weight_out[j] = jnp.where(row <= col, jnp.exp(now[j : j + 1] - tall[:, j : j + 1]), 0.0)
        cols = slice(j * width, (j + 1) * width)
        keyt_out[j] = keys[:, cols].T
        ridge_out[j] = jnp.broadcast_to(ridge[j : j + 1], (width, width)).T
        q = queries[:, cols].astype(F).T
        query_out[j] = q * lax.rsqrt(jnp.sum(q * q, axis=0, keepdims=True) + 1e-06)


def weights_call(count, keys, queries, run, square, ridge, width, chunk):
    tokens = queries.shape[0]
    heads = run.shape[0]
    shapes = [
        jax.ShapeDtypeStruct((heads, tokens, tokens), F),
        jax.ShapeDtypeStruct((heads, width, tokens), F),
        jax.ShapeDtypeStruct((heads, width, tokens), B),
        jax.ShapeDtypeStruct((heads, width, width), F),
    ]
    block = spec((tokens, chunk * width), lambda i: (0, i))
    return pl.pallas_call(
        functools.partial(weights_kernel, chunk, width),
        grid=(heads // chunk,),
        in_specs=[
            SMEM,
            block,
            block,
            stack(run, chunk),
            stack(square, chunk),
            stack(ridge, chunk),
        ],
        out_specs=[stack(s, chunk) for s in shapes],
        out_shape=shapes,
        scratch_shapes=[pltpu.VMEM((128, tokens), F)],
        compiler_params=params(20),
        cost_estimate=cost(2),
        name="weights",
    )(count, keys, queries, run, square, ridge)


def solve_kernel(
    chunk, width, base, opening, coarse, me, keys, keyt, queries, weights, run, ridge, *rest
):
    tokens = keys.shape[0]
    half_t = tokens // 2
    c = me[0] & 1
    if opening:
        mine, theirs, first, start, answer_out, left, dirs, resid, norm_out, *rest = rest
    else:
        answer_in, left, dirs_in, resid_in, norm_in, answer_out, dirs, resid, *rest = rest
    near_top, near_low, far = rest
    lead = []
    norms = []
    for j in range(chunk):
        lead.append(jnp.exp(run[j : j + 1, :]))
        if not opening:
            dirs[j] = dirs_in[j]
            resid[j] = resid_in[j]
            answer_out[j] = answer_in[j]
            norms.append(norm_in[j : j + 1, :])
            continue
        key = keys[:, j * width : (j + 1) * width]
        left[j, :tokens, :width] = key
        left[j, :tokens, width:] = key
        gram = state_of(c, base + j, width // 2 + 1, mine, theirs, first, start[j]).astype(B)
        left[j, tokens:, :width] = gram
        left[j, tokens:, width:] = gram
        q = queries[j]
        dirs[j] = q
        resid[j] = q
        answer_out[j] = jnp.zeros_like(q)
        norms.append(jnp.sum(q * q, axis=0, keepdims=True))

    def spread(j, fine):
        p = dirs[j]
        if fine:
            hi, lo = split(p)
            image = dot(left[j], jnp.concatenate([hi, lo], 0))
        else:
            image = dot(left[j, :, :width], p.astype(B))
        far[j] = image[tokens:]
        top = image[:half_t] * weights[j, :half_t]
        low = image[half_t:tokens, half_t:] * weights[j, half_t:, half_t:]
        if fine:
            near_top[j, 0], near_top[j, 1] = split(top)
            near_low[j, 0], near_low[j, 1] = split(low)
        else:
            near_top[j, 0] = top.astype(B)
            near_low[j, 0] = low.astype(B)

    def gather(j, fine, norm):
        kt = keyt[j]
        p = dirs[j]
        if fine:
            early = kt[:, :half_t]
            one = dot(
                jnp.concatenate([early, early], 1),
                jnp.concatenate([near_top[j, 0, :, :half_t], near_top[j, 1, :, :half_t]], 0),
            )
            two = dot(
                kt,
                jnp.concatenate(
                    [
                        jnp.concatenate([near_top[j, 0, :, half_t:], near_top[j, 1, :, half_t:]], 1),
                        jnp.concatenate([near_low[j, 0], near_low[j, 1]], 1),
                    ],
                    0,
                ),
            )
            near = jnp.concatenate([one, two[:, :half_t] + two[:, half_t:]], 1)
        else:
            low = near_low[j, 0]
            near = dot(
                kt,
                jnp.concatenate(
                    [near_top[j, 0], jnp.concatenate([jnp.zeros_like(low), low], 1)], 0
                ),
            )
        image = lead[j] * far[j] + near + jnp.concatenate([ridge[j]] * (tokens // width), 1) * p
        step = norm / jnp.sum(p * image, axis=0, keepdims=True)
        answer_out[j] = answer_out[j] + step * p
        r = resid[j] - step * image
        resid[j] = r
        after = jnp.sum(r * r, axis=0, keepdims=True)
        dirs[j] = r + (after / norm) * p
        return after

    cut = max(chunk // 2, 1)
    pairs = list(zip(range(cut), range(cut, chunk)))

    def turn(fine, then):
        def body(_, norms):
            norms = list(norms)
            for a, b in pairs:
                spread(b, fine)
                norms[a] = gather(a, fine, norms[a])
            for a, b in pairs:
                if then is not None:
                    spread(a, then)
                norms[b] = gather(b, fine, norms[b])
            return tuple(norms)

        return body

    kinds = ([(True, FINE)] if opening else []) + ([(False, coarse)] if coarse else [])
    for a, _ in pairs:
        spread(a, kinds[0][0])
    norms = tuple(norms)
    for n, (kind, turns) in enumerate(kinds):
        norms = lax.fori_loop(0, turns - 1, turn(kind, kind), norms, unroll=4)
        norms = turn(kind, kinds[n + 1][0] if n + 1 < len(kinds) else None)(0, norms)
    if opening:
        for j in range(chunk):
            norm_out[j : j + 1, :] = norms[j]


def solve_call(
    me, keys, keyt, queries, weights, run, ridge, rest, start, coarse, chunk, place
):
    opening = start is not None
    tokens = keys.shape[0]
    width = keyt.shape[1]

    def mine(a):
        zeros = (0,) * (a.ndim - 1)
        return spec((chunk, *a.shape[1:]), lambda i: (place, *zeros))

    block = spec((tokens, chunk * width), lambda i: (0, place))
    ins = [me, keys, keyt, queries, weights, run, ridge, *rest]
    in_specs = (
        [SMEM, block]
        + [mine(a) for a in ins[2:7]]
        + [whole(a.shape) for a in rest]
    )
    columns = jax.ShapeDtypeStruct((chunk, width, tokens), F)
    state = pltpu.VMEM((chunk, width, tokens), F)
    if opening:
        ins.append(start)
        in_specs.append(spec((chunk, width, width), lambda i: (place, 0, 0)))
        shapes = [
            columns,
            jax.ShapeDtypeStruct((chunk, tokens + width, 2 * width), B),
            columns,
            columns,
            jax.ShapeDtypeStruct((chunk, tokens), F),
        ]
        scratch = []
    else:
        shapes = [columns]
        scratch = [state, state]
    return pl.pallas_call(
        functools.partial(solve_kernel, chunk, width, 0, opening, coarse),
        grid=(1,),
        in_specs=in_specs,
        out_specs=[whole(s.shape) for s in shapes],
        out_shape=shapes,
        scratch_shapes=scratch
        + [
            pltpu.VMEM((chunk, 2, tokens // 2, tokens), B),
            pltpu.VMEM((chunk, 2, tokens // 2, tokens // 2), B),
            state,
        ],
        compiler_params=params(30),
        cost_estimate=cost(11 if opening else 9),
        name="solve_fine" if opening else "solve",
    )(*ins)


def readout_kernel(
    width, batch, parts, me, keys, values, weights, run, square, gain,
    mine, theirs, first, start, out_weight, count, *rest
):
    answers = rest[:parts]
    out, total = rest[parts:]
    tokens = keys.shape[0]
    i = pl.program_id(0)
    turns = pl.num_programs(0)
    c = me[0] & 1

    @pl.when(i == 0)
    def _():
        total[...] = jnp.zeros_like(total)

    at = lax.broadcasted_iota(jnp.int32, (1, tokens), 1)
    live = (at < count[0]).astype(F)
    rows = []
    for j in range(batch):
        cols = slice(j * width, (j + 1) * width)
        head = i * batch + j
        line = pl.ds(head, 1)
        answer = answers[0][j]
        for n in range(1, parts):
            answer = jnp.where(i * parts < n * turns, answer, answers[n][j])
        hi, lo = split(answer)
        both = jnp.concatenate([hi, lo], 0)
        key = keys[:, cols]
        near = (dot(jnp.concatenate([key, key], 1), both) * weights[j]).astype(B)
        value = (values[:, cols].astype(F).T * jnp.sqrt(square[line, :])).astype(B)
        memory = state_of(c, head, width, mine, theirs, first, start[j]).astype(B)
        o = jnp.exp(run[line, :]) * dot(jnp.concatenate([memory, memory], 1), both) + dot(value, near)
        scale = lax.rsqrt(jnp.mean(o * o, axis=0, keepdims=True) + 1e-05) * live
        rows.append((o * scale).T * gain[:, cols])
    y = jnp.concatenate(rows, 1).astype(B)
    total[...] += dot(y, out_weight[...])

    @pl.when(i == turns - 1)
    def _():
        out[...] = total[...].astype(B)


def readout_call(
    me, keys, values, answers, weights, run, square, gain, state, start, out_weight, count
):
    tokens = keys.shape[0]
    heads = run.shape[0]
    chunk, width, _ = answers[0].shape
    model = out_weight.shape[1]
    batch = min(chunk, BATCH)
    each = chunk // batch
    tok = spec((tokens, batch * width), lambda i: (0, i))
    ins = [me, keys, values, weights, run, square, gain.reshape(1, -1), *state, start,
           out_weight, count, *answers]

    def part(n):
        return spec(
            (batch, width, tokens), lambda i: (jnp.clip(i - n * each, 0, each - 1), 0, 0)
        )

    in_specs = [
        SMEM,
        tok,
        tok,
        stack(weights, batch),
        whole(run.shape),
        whole(square.shape),
        spec((1, batch * width), lambda i: (0, i)),
        *[whole(a.shape) for a in state],
        stack(start, batch),
        spec((batch * width, model), lambda i: (i, 0)),
        SMEM,
        *[part(n) for n in range(len(answers))],
    ]
    return pl.pallas_call(
        functools.partial(readout_kernel, width, batch, len(answers)),
        grid=(heads // batch,),
        in_specs=in_specs,
        out_specs=whole((tokens, model)),
        out_shape=jax.ShapeDtypeStruct((tokens, model), B),
        scratch_shapes=[pltpu.VMEM((tokens, model), F)],
        compiler_params=params(30),
        cost_estimate=cost(7),
        name="readout",
    )(*ins)


def local(
    shards, columns,
    queries, key_vectors, value_vectors, forget_gates, shard_counts, gram_start,
    memory_start, ridge_terms, norm_gain, out_weight,
):
    heads = forget_gates.shape[1]
    width = queries.shape[1] // heads
    chunk = min(heads, 8)
    parts = range(heads // chunk)
    me = lax.axis_index("seq").astype(jnp.int32).reshape(1)
    gates = forget_gates.T
    sums = [gram_call(shard_counts, gates, key_vectors, chunk, n) for n in parts]
    run = jnp.concatenate([a[2] for a in sums], 0)
    square = jnp.concatenate([a[3] for a in sums], 0)

    grams = [Run(prefix(me, a[0], a[1], width // 2 + 1, shards)) for a in sums]

    def advance(*late):
        for g in grams:
            if g.state is None:
                g.step(*[o.sent for o in grams if o is not g], *(late if g is grams[-1] else ()))

    advance()
    values = after(value_vectors, *[g.sent for g in grams])
    memories = memory_call(shard_counts, run, square, key_vectors, values, width, chunk)
    memory = Run(prefix(me, *memories, width, shards))
    advance()
    memory.step(grams[-1].sent)
    advance(memory.sent)
    weights, vectors, keyt, ridge = weights_call(
        shard_counts, key_vectors, after(queries, grams[0].sent), run, square, ridge_terms, width,
        chunk,
    )
    advance(vectors)
    memory.step(grams[-1].sent)
    states = [grams[0].finish(*[g.sent for g in grams[1:]], memory.sent)]

    answers = []
    last = memory.sent
    for n in parts:
        common = (weights, run, ridge)
        early = EARLY if n == len(parts) - 1 else 0
        opened = solve_call(
            me, key_vectors, keyt, after(vectors, last, memory.sent, *[g.sent for g in grams]), *common,
            states[n], gram_start, early, chunk, n,
        )
        opened = list(opened)
        states += [g.finish(opened[0]) for g in grams[n + 1 : n + 2]]
        if memory.state is None:
            memory.step(opened[0])
            opened[0] = after(opened[0], memory.sent)
        answers += solve_call(
            me, key_vectors, keyt, vectors, *common, opened, None, ITERS - FINE - early, chunk, n
        )
        last = answers[-1]
        if n == 0 and memory.state is None:
            memory.step(last)
    memory_state = memory.finish(last)
    mixed = readout_call(
        me, key_vectors, value_vectors, answers, weights, run, square, norm_gain,
        memory_state, memory_start, out_weight, shard_counts,
    )
    if columns > 1:
        mixed = lax.psum_scatter(mixed, "head", scatter_dimension=1, tiled=True)
    return mixed


def solution(mesh):
    return jax.shard_map(
        functools.partial(local, mesh.shape["seq"], mesh.shape["head"]),
        mesh=mesh,
        in_specs=(
            P("seq", "head"),
            P("seq", "head"),
            P("seq", "head"),
            P("seq", "head"),
            P("seq"),
            P("head", None, None),
            P("head", None, None),
            P("head", None),
            P("head"),
            P("head", None),
        ),
        out_specs=P("seq", "head"),
        check_vma=False,
    )
```
